512 devices in a mesh: row: 32 (over z, y_hi), mem: 8 (over x, core), lev: 2 (over y_lo).
Axes of the slice: x: 4, y: 8 (y_hi: 4, y_lo: 2; y = y_hi * 2 + y_lo), z: 8, core: 2. Of those that a mesh axis runs over, the one named last changes fastest.
Arguments:
- control_fields: bfloat16 [16, 6, 1024, 2048], P('mem', 'lev', 'row'), may hold values from -6 to 6
- perturbations: bfloat16 [3, 16, 6, 1024, 2048], P(None, 'mem', 'lev', 'row'), may hold values from -1.5 to 1.5
- column_taper: bfloat16 [2048, 2048], P('row'), may hold values from -1 to 2, as said below
- row_taper: bfloat16 [1024, 1024], P('row'), may hold values from -1 to 2, as said below
- courant_numbers: float32 [3, 6, 1024, 2048], P(None, 'lev', 'row', 'mem'), may hold values from -0.3 to 0.3
- tracer_slope: float32 [2, 6, 1024, 2048], P(None, 'lev', 'row', 'mem'), may hold values from -3 to 3
Outputs:
- increment: float32 [3, 6, 1024, 2048], P(None, 'lev', 'row', 'mem')
The draws below stay inside these ranges and needn't reach their ends.
Inputs may be any that keep to these rules, and one draw needn't show every extreme that they name: `column_taper`: A square matrix. `row_taper`: A square matrix.
All inputs are finite; a program needn't handle non-finite values.
Results may differ from the reference program's by a relative error of at most 0.0048.
Values may be sent and summed in bfloat16 or wider, within the bound.
No kernel may reach another device: no remote copies, remote signals or barrier semaphores. Data moves between devices by JAX's collectives and lax.ppermute only.
A program may use at most 64 MiB of HBM per device.

```python
import jax
import jax.numpy as jnp
from jax import lax

NX = 2048
STEPS = 4
NY = 1024
M = 16
LEV = 6


def banded(key, order):
    first_index = jnp.arange(order)[:, None]
    second_index = jnp.arange(order)[None, :]
    reach = order / 4.0
    noise = jnp.clip(jax.random.normal(key, (order, order), jnp.float32), -4.0, 4.0)
    distance = jnp.abs(first_index - second_index).astype(jnp.float32)
    diagonal = jnp.where(first_index == second_index, 1.0, 0.0).astype(jnp.float32)
    return (diagonal + noise * jnp.exp(-distance / reach) / jnp.sqrt(reach)).astype(jnp.bfloat16)


def draw_column_taper(key, part):
    return banded(jax.random.fold_in(key, 11), NX)


def draw_row_taper(key, part):
    return banded(jax.random.fold_in(key, 23), NY)


def level_of(own_key, shape, pieces, low, top_value):
    gain = 1.0
    for axis_at, parts in pieces:
        heights = jax.random.uniform(jax.random.fold_in(jax.random.fold_in(own_key, 6), axis_at), (parts,), jnp.float32, low / len(pieces), top_value / len(pieces))
        gain = gain * jnp.repeat(jnp.exp(heights), shape[axis_at] // parts).reshape((-1,) + (1,) * (len(shape) - 1 - axis_at))
    return gain


def scatter_about(own_key, dims, width, bound, split=(), held_as=jnp.bfloat16):
    array = jax.random.normal(own_key, dims, jnp.float32) * width
    if len(split) > 0:
        array = level_of(own_key, dims, split, -0.22, 0.18) * array
    return jnp.clip(array, min=-bound, max=bound).astype(held_as)


def setup_inputs(seed: int = 0) -> dict:
    key_list = jax.random.split(jax.random.key(seed), 7)
    return {
        "control_fields": scatter_about(key_list[0], (M, LEV, NY, NX), 1.0, 6.0, ((0, 8), (1, 2), (2, 32))),
        "perturbations": scatter_about(key_list[1], (3, M, LEV, NY, NX), M ** -0.5, 1.5, ((1, 8), (2, 2), (3, 32))),
        "column_taper": draw_column_taper(jax.random.fold_in(key_list[6], 71), 0),
        "row_taper": draw_row_taper(jax.random.fold_in(key_list[6], 71), 0),
        "courant_numbers": jnp.clip(jax.random.uniform(key_list[4], (3, LEV, NY, NX), jnp.float32, -0.3, 0.3) * level_of(key_list[4], (3, LEV, NY, NX), ((1, 2), (2, 32), (3, 8)), -0.4, 0.0), -0.3, 0.3),
        "tracer_slope": scatter_about(key_list[5], (2, LEV, NY, NX), 0.5, 3.0, ((1, 2), (2, 32), (3, 8)), jnp.float32),
    }


def upwind(middle, behind, forward, velocity):
    return jnp.maximum(velocity, 0.0) * (middle - behind) + jnp.minimum(velocity, 0.0) * (forward - middle)


def advance(present, courant_numbers, tracer_slope, padded):
    middle = padded[:, 1:-1, 1:-1, 1:-1]
    change = upwind(middle, padded[:, :-2, 1:-1, 1:-1], padded[:, 2:, 1:-1, 1:-1], courant_numbers[0])
    change = change + upwind(middle, padded[:, 1:-1, :-2, 1:-1], padded[:, 1:-1, 2:, 1:-1], courant_numbers[1])
    change = change + upwind(middle, padded[:, 1:-1, 1:-1, :-2], padded[:, 1:-1, 1:-1, 2:], courant_numbers[2])
    shifted = present - change
    source = present[0] * tracer_slope[0] + present[1] * tracer_slope[1]
    return jnp.concatenate([shifted[:2], shifted[2:] - source[None]], axis=0)


def reference(control_fields, perturbations, column_taper, row_taper, courant_numbers, tracer_slope):
    def per_level(plane):
        first_pass = jnp.dot(plane, column_taper, preferred_element_type=jnp.float32).astype(jnp.bfloat16)
        return jnp.dot(row_taper, first_pass, preferred_element_type=jnp.float32).astype(jnp.bfloat16)

    def accumulate(running, member_pair):
        control_one, perturb_one = member_pair
        localized = lax.map(per_level, control_one)
        return running + perturb_one.astype(jnp.float32) * localized.astype(jnp.float32)[None], None

    starting = jnp.zeros((3,) + control_fields.shape[1:], jnp.float32)
    present, ignored = lax.scan(accumulate, starting, (control_fields, jnp.moveaxis(perturbations, 1, 0)))
    for advect_step in range(STEPS):
        padded = jnp.pad(present, ((0, 0), (1, 1), (1, 1), (1, 1)))
        present = advance(present, courant_numbers, tracer_slope, padded)
    return present
```

```python
import jax
import jax.numpy as jnp
from jax import lax
from jax.experimental import pallas as pl
from jax.experimental.pallas import tpu as pltpu
from jax.sharding import PartitionSpec as P

STEPS = 4
BF = jnp.bfloat16
F32 = jnp.float32


def room(mebibytes):
    return pltpu.CompilerParams(vmem_limit_bytes=mebibytes * 1024 * 1024)


def in_hbm(x):
    return pltpu.with_memory_space_constraint(x, pltpu.HBM)


def shaped(shape, dtype):
    return jax.ShapeDtypeStruct(shape, dtype)


def slices_kernel(_, column_ref, row_ref, out_ref):
    tall = column_ref.shape[0]
    half = row_ref.shape[0] // 2
    wide = row_ref.shape[1]
    peers = out_ref.shape[0]
    out_ref[:, :tall, :] = jnp.broadcast_to(column_ref[...][None], (peers, *column_ref.shape))
    upper, lower = (row_ref[:half, :], row_ref[half:, :])
    out_ref[:, tall:, :wide] = jnp.broadcast_to(upper[None], (peers, half, wide))
    out_ref[:, tall:, wide:] = jnp.broadcast_to(lower[None], (peers, half, wide))


def taper_slices(at, column_taper, row_taper, peers, parts):
    tall, wide = (column_taper.shape[0], column_taper.shape[1] // parts)
    rows, narrow = (row_taper.shape[0], row_taper.shape[1] // parts)
    return pl.pallas_call(
        slices_kernel,
        out_shape=shaped((peers, tall + rows // 2, wide), BF),
        grid_spec=pltpu.PrefetchScalarGridSpec(
            num_scalar_prefetch=1,
            grid=(1,),
            in_specs=[
                pl.BlockSpec((tall, wide), lambda i, at: (0, at[0])),
                pl.BlockSpec((rows, narrow), lambda i, at: (0, at[0])),
            ],
            out_specs=pl.BlockSpec((peers, tall + rows // 2, wide), lambda i, at: (0, 0, 0)),
        ),
        compiler_params=room(6),
        name="taper_slices",
    )(at, column_taper, row_taper)


def row_part_kernel(tall, slices_ref, out_ref):
    half = slices_ref.shape[1] - tall
    wide = out_ref.shape[2]
    out_ref[:, :half, :] = slices_ref[:, tall:, :wide]
    out_ref[:, half:, :] = slices_ref[:, tall:, wide:]


def row_part(slices, tall, settled):
    peers, height, wide = slices.shape
    return pl.pallas_call(
        lambda a, *rest: row_part_kernel(tall, a, rest[-1]),
        out_shape=shaped((peers, 2 * (height - tall), wide // 2), BF),
        in_specs=[pl.BlockSpec(memory_space=pltpu.VMEM)]
        + [pl.BlockSpec(memory_space=pl.ANY)] * len(settled),
        compiler_params=room(4),
        name="row_part",
    )(slices, *settled)


def columns_kernel(tall, fields_ref, slices_ref, out_ref):
    units, levels, rows, wide = out_ref.shape
    taper = slices_ref[:, :tall, :].reshape(-1, slices_ref.shape[2])
    product = jnp.dot(fields_ref[...], taper, preferred_element_type=F32).astype(BF)
    for member in range(units // 2):
        for side in range(2):
            part = product[
                member * levels * rows : (member + 1) * levels * rows,
                side * wide : (side + 1) * wide,
            ]
            out_ref[member * 2 + side] = part.reshape(levels, rows, wide)


def columns_pass(fields, slices, tall, levels, rows, parts):
    count, depth = fields.shape
    peers, height, wide = slices.shape
    units = 2 * count // (levels * rows)
    return pl.pallas_call(
        lambda a, b, c: columns_kernel(tall, a, b, c),
        out_shape=shaped((units, levels, rows, wide // 2), BF),
        grid=(parts,),
        in_specs=[
            pl.BlockSpec((count // parts, depth), lambda i: (i, 0)),
            pl.BlockSpec((peers, height, wide), lambda i: (0, 0, 0)),
        ],
        out_specs=pl.BlockSpec((units // parts, levels, rows, wide // 2), lambda i: (i, 0, 0, 0)),
        compiler_params=room(14),
        name="columns_pass",
    )(in_hbm(fields), slices)


def rows_kernel(taper_ref, fields_ref, *refs):
    out_ref, whole_ref = refs[-2:]
    peers, levels, rows, wide = fields_ref.shape

    @pl.when(pl.program_id(0) == 0)
    def _():
        for level in range(levels):
            whole_ref[:, level * wide : (level + 1) * wide] = fields_ref[:, level].reshape(
                peers * rows, wide
            )

    taper = jnp.concatenate([taper_ref[i] for i in range(taper_ref.shape[0])], axis=1)
    product = jnp.dot(taper, whole_ref[...], preferred_element_type=F32).astype(BF)
    for level in range(levels):
        out_ref[:, level] = product[:, level * wide : (level + 1) * wide].reshape(-1, rows, wide)


def rows_pass(taper, fields, blocks, settled):
    peers, levels, rows, wide = fields.shape
    parts, height, narrow = taper.shape
    return pl.pallas_call(
        rows_kernel,
        out_shape=shaped((peers, levels, rows, wide), BF),
        grid=(blocks,),
        in_specs=[
            pl.BlockSpec((parts, height // blocks, narrow), lambda i: (0, i, 0)),
            pl.BlockSpec((peers, levels, rows, wide), lambda i: (0, 0, 0, 0)),
        ]
        + [pl.BlockSpec(memory_space=pl.ANY)] * len(settled),
        out_specs=pl.BlockSpec((peers // blocks, levels, rows, wide), lambda i: (i, 0, 0, 0)),
        scratch_shapes=[pltpu.VMEM((height, levels * wide), BF)],
        compiler_params=room(10),
        name="rows_pass",
    )(in_hbm(taper), fields, *settled)


def split_kernel(at_ref, fields_ref, *out_refs):
    wide = out_refs[0].shape[-1]
    for step, out_ref in enumerate(out_refs):
        start = pl.multiple_of((at_ref[0] ^ step) * wide, wide)
        out_ref[...] = fields_ref[:, :, :, :, pl.ds(start, wide)]


def split_columns(at, fields, parts):
    shape = (*fields.shape[:-1], fields.shape[-1] // parts)
    return pl.pallas_call(
        split_kernel,
        out_shape=[shaped(shape, BF)] * parts,
        in_specs=[
            pl.BlockSpec(memory_space=pltpu.SMEM),
            pl.BlockSpec(memory_space=pltpu.VMEM),
        ],
        out_specs=[pl.BlockSpec(memory_space=pltpu.VMEM)] * parts,
        compiler_params=room(8),
        name="split_columns",
    )(at, fields)


def weight_kernel(parts, at_ref, localized_ref, *refs):
    weights = refs[:parts]
    out_ref, whole_ref, first_ref, last_ref = refs[parts:]
    variables, members, levels = weights[0].shape[:3]
    wide = localized_ref.shape[-1]
    for level in range(levels):
        for side in range(2):
            lanes = slice(side * wide, (side + 1) * wide)
            sums = [None] * variables
            for step in range(parts):
                base = (at_ref[0] ^ step) * (2 * members)
                for member in range(members):
                    field = localized_ref[base + 2 * member + side, level].astype(F32)
                    for k in range(variables):
                        term = weights[step][k, member, level, :, lanes].astype(F32) * field
                        sums[k] = term if sums[k] is None else sums[k] + term
            for k in range(variables):
                out_ref[k, level, :, lanes] = sums[k]
                rounded = sums[k].astype(BF)
                whole_ref[k, level, :, lanes] = rounded
                (first_ref, last_ref)[side][k, level] = rounded


def weighted_sum(at, localized, weights):
    variables, _, levels, rows, wide = weights[0].shape
    shape = (variables, levels, rows, wide)
    edge = (variables, levels, rows, wide // 2)
    vmem = pl.BlockSpec(memory_space=pltpu.VMEM)
    return pl.pallas_call(
        lambda *refs: weight_kernel(len(weights), *refs),
        out_shape=[shaped(shape, F32), shaped(shape, BF), shaped(edge, BF), shaped(edge, BF)],
        in_specs=[pl.BlockSpec(memory_space=pltpu.SMEM)] + [vmem] * (1 + len(weights)),
        out_specs=[vmem] * 4,
        compiler_params=room(8),
        name="weighted_sum",
    )(at, localized, *weights)


def beside(from_left, from_right):
    lane = lax.broadcasted_iota(jnp.int32, from_left.shape, from_left.ndim - 1)
    wide = from_left.shape[-1]
    none = jnp.zeros_like(from_left)
    kept = jnp.where(lane >= wide - STEPS, from_left, none)
    return jnp.where(lane < STEPS, from_right, kept)


def above_below(from_next, from_previous):
    row = lax.broadcasted_iota(jnp.int32, from_next.shape, from_next.ndim - 2)
    return jnp.where(row < STEPS, from_next, from_previous)


def strips_kernel(own_ref, other_ref, *refs):
    (left, right, other_left, other_right), (top_ref, bottom_ref) = (refs[:4], refs[4:])
    variables, levels, rows, wide = own_ref.shape
    for rows_at, out_ref in ((slice(0, 8), top_ref), (slice(rows - 8, rows), bottom_ref)):
        for k in range(variables):
            for level in range(levels):
                for base, body, l_ref, r_ref in (
                    (0, own_ref, left, right),
                    (levels, other_ref, other_left, other_right),
                ):
                    out_ref[k, base + level, :, :wide] = body[k, level, rows_at]
                    sides = beside(
                        l_ref[k, level, rows_at].astype(F32), r_ref[k, level, rows_at].astype(F32)
                    )
                    out_ref[k, base + level, :, wide:] = sides.astype(BF)


def row_strips(own, other, *sides):
    variables, levels, rows, wide = own.shape
    shape = (variables, 2 * levels, 8, wide + sides[0].shape[-1])
    return pl.pallas_call(
        strips_kernel,
        out_shape=[shaped(shape, BF)] * 2,
        compiler_params=room(4),
        name="row_strips",
    )(own, other, *sides)


def advect_kernel(*refs):
    (
        flip_ref,
        own_ref,
        other_ref,
        left_ref,
        right_ref,
        other_left_ref,
        other_right_ref,
        next_ref,
        previous_ref,
        courant_ref,
        slope_ref,
        beside_ref,
        around_ref,
        opposite_ref,
        out_ref,
        first_ref,
        second_ref,
        terms_ref,
    ) = refs
    variables, levels, rows, wide = own_ref.shape
    deep, tall, full = first_ref.shape[1:]
    flip = flip_ref[0]
    sign = (1 - 2 * flip).astype(F32)
    directions = courant_ref.shape[0]

    def local(level):
        return jnp.where(flip == 1, levels - 1 - level, level)

    for level in range(deep):
        at = local(level % levels)
        mine = level < levels
        for k in range(variables):
            body, l_ref, r_ref = (
                (own_ref, left_ref, right_ref)
                if mine
                else (other_ref, other_left_ref, other_right_ref)
            )
            first_ref[k, level, :rows, :wide] = body[k, at].astype(F32)
            first_ref[k, level, :rows, wide:] = beside(
                l_ref[k, at].astype(F32), r_ref[k, at].astype(F32)
            )
            strip = at if mine else at + levels
            first_ref[k, level, rows:, :] = above_below(
                next_ref[k, strip].astype(F32), previous_ref[k, strip].astype(F32)
            )
        planes = []
        for a in range(directions + slope_ref.shape[0]):
            if mine:
                body = courant_ref[a, at] if a < directions else slope_ref[a - directions, at]
                upper = jnp.concatenate([body, beside_ref[a, at].astype(F32)], axis=1)
                plane = jnp.concatenate([upper, around_ref[a, at].astype(F32)], axis=0)
            else:
                plane = opposite_ref[a, at].astype(F32)
            planes.append(plane)
        planes[0] = planes[0] * sign
        kept = 1.0 - sum(jnp.abs(c) for c in planes[:directions])
        terms_ref[0, level] = kept
        for a in range(directions):
            terms_ref[1 + 2 * a, level] = jnp.maximum(planes[a], 0.0)
            terms_ref[2 + 2 * a, level] = -jnp.minimum(planes[a], 0.0)
        for a in range(directions, len(planes)):
            terms_ref[1 + directions + a, level] = planes[a]

    old_ref, new_ref = (first_ref, second_ref)
    for step in range(STEPS):
        reached = min(deep, levels + STEPS - 1 - step)
        last = step == STEPS - 1
        for level in range(reached):
            states = [old_ref[k, level] for k in range(variables)]
            for k in range(variables):
                state = states[k]
                total = terms_ref[0, level] * state
                if level > 0:
                    total = total + terms_ref[1, level] * old_ref[k, level - 1]
                if level + 1 < deep:
                    total = total + terms_ref[2, level] * old_ref[k, level + 1]
                total = total + terms_ref[3, level] * pltpu.roll(state, 1, 0)
                total = total + terms_ref[4, level] * pltpu.roll(state, tall - 1, 0)
                total = total + terms_ref[5, level] * pltpu.roll(state, 1, 1)
                total = total + terms_ref[6, level] * pltpu.roll(state, full - 1, 1)
                if k == 2:
                    total = total - (states[0] * terms_ref[7, level] + states[1] * terms_ref[8, level])
                if last:
                    out_ref[k, local(level)] = total[:rows, :wide]
                else:
                    new_ref[k, level] = total
        old_ref, new_ref = (new_ref, old_ref)


def advect(flip, *arrays):
    variables, levels, rows, wide = arrays[0].shape
    tall, full = (rows + 8, wide + arrays[2].shape[-1])
    vmem = pl.BlockSpec(memory_space=pltpu.VMEM)
    state = pltpu.VMEM((variables, 2 * levels, tall, full), F32)
    return pl.pallas_call(
        advect_kernel,
        out_shape=shaped((variables, levels, rows, wide), F32),
        in_specs=[pl.BlockSpec(memory_space=pltpu.SMEM)] + [vmem] * len(arrays),
        out_specs=vmem,
        scratch_shapes=[state, state, pltpu.VMEM((9, 2 * levels, tall, full), F32)],
        compiler_params=room(14),
        name="advect",
    )(flip, *arrays)


def chain(axis, step):
    size = lax.axis_size(axis)
    return [(i, i + step) for i in range(size) if 0 <= i + step < size]


def swap(axis):
    return [(0, 1), (1, 0)]


def neighbours(first, last, axis):
    from_left = lax.ppermute(last, axis, chain(axis, 1))
    from_right = lax.ppermute(first, axis, chain(axis, -1))
    return from_left, from_right


def across(first, last):
    size = lax.axis_size("mem")
    up = [(2 * i + k, 2 * (i + 1) + 1 - k) for i in range(size - 1) for k in range(2)]
    down = [(2 * (i + 1) + k, 2 * i + 1 - k) for i in range(size - 1) for k in range(2)]
    axes = ("mem", "lev")
    return lax.ppermute(last, axes, up), lax.ppermute(first, axes, down)


def background(courant_numbers, tracer_slope):
    whole = jnp.concatenate([courant_numbers, tracer_slope], axis=0).astype(BF)
    half = whole.shape[-1] // 2
    sides = beside(*neighbours(whole[..., :half], whole[..., half:], "mem"))
    wider = jnp.concatenate([whole, sides], axis=-1)
    from_previous, from_next = neighbours(wider[:, :, :8], wider[:, :, -8:], "row")
    around = above_below(from_next, from_previous)
    taller = jnp.concatenate([wider, around], axis=2)
    return sides, around, lax.ppermute(taller, "lev", swap("lev"))


def on_device(
    control_fields, perturbations, column_taper, row_taper, courant_numbers, tracer_slope
):
    members, levels, rows, columns = control_fields.shape
    parts, peers = (lax.axis_size("mem"), lax.axis_size("row"))
    tall = column_taper.shape[0]
    at = lax.axis_index("mem").astype(jnp.int32).reshape(1)
    flip = lax.axis_index("lev").astype(jnp.int32).reshape(1)

    every = lax.all_gather(
        control_fields.reshape(members * levels * rows, columns), "mem", axis=0, tiled=True
    )
    slices = lax.all_to_all(
        taper_slices(at, column_taper, row_taper, peers, parts), "row", 0, 0, tiled=True
    )
    sides, around, opposite = background(courant_numbers, tracer_slope)
    pieces = split_columns(at, perturbations, parts)
    weights = [pieces[0]]
    for step in range(1, parts):
        weights.append(lax.ppermute(pieces[step], "mem", [(i, i ^ step) for i in range(parts)]))
    first_pass = columns_pass(every, slices, tall, levels, rows, 4)
    row_whole = lax.all_gather(row_part(slices, tall, weights[1:]), "mem", axis=0, tiled=False)
    row_whole = row_whole.reshape(parts, row_taper.shape[1], -1)
    arrived = lax.all_to_all(first_pass, "row", 0, 0, tiled=True)
    tapered = rows_pass(row_whole, arrived, 4, [opposite])
    localized = lax.all_to_all(tapered, "row", 0, 0, tiled=True)
    own, rounded, first, last = weighted_sum(at, localized, weights)

    other = lax.ppermute(rounded, "lev", swap("lev"))
    left, right = neighbours(first, last, "mem")
    other_left, other_right = across(first, last)
    top, bottom = row_strips(rounded, other, left, right, other_left, other_right)
    from_previous, from_next = neighbours(top, bottom, "row")
    return advect(
        flip,
        own,
        other,
        left,
        right,
        other_left,
        other_right,
        from_next,
        from_previous,
        courant_numbers,
        tracer_slope,
        sides,
        around,
        opposite,
    )


def solution(mesh):
    grid = P(None, "lev", "row", "mem")
    placed = (
        P("mem", "lev", "row", None),
        P(None, "mem", "lev", "row", None),
        P("row", None),
        P("row", None),
        grid,
        grid,
    )
    return jax.shard_map(
        on_device, mesh=mesh, in_specs=placed, out_specs=grid, check_vma=False
    )
```

```python
import jax
import jax.numpy as jnp
from jax import lax
from jax.experimental import pallas as pl
from jax.experimental.pallas import tpu as pltpu
from jax.sharding import PartitionSpec as P

STEPS = 4
BF = jnp.bfloat16
F32 = jnp.float32


def room(mebibytes):
    return pltpu.CompilerParams(vmem_limit_bytes=mebibytes * 1024 * 1024)


def in_hbm(x):
    return pltpu.with_memory_space_constraint(x, pltpu.HBM)


def shaped(shape, dtype):
    return jax.ShapeDtypeStruct(shape, dtype)


def after(arrays, settled):
    count = len(arrays)
    anywhere = pl.BlockSpec(memory_space=pl.ANY)
    return pl.pallas_call(
        lambda *refs: None,
        out_shape=[shaped(x.shape, x.dtype) for x in arrays],
        in_specs=[anywhere] * (count + len(settled)),
        out_specs=[anywhere] * count,
        input_output_aliases={i: i for i in range(count)},
        name="after",
    )(*arrays, *settled)


def slices_kernel(_, column_ref, row_ref, out_ref):
    tall = column_ref.shape[0]
    half = row_ref.shape[0] // 2
    wide = row_ref.shape[1]
    peers = out_ref.shape[0]
    out_ref[:, :tall, :] = jnp.broadcast_to(column_ref[...][None], (peers, *column_ref.shape))
    upper, lower = (row_ref[:half, :], row_ref[half:, :])
    out_ref[:, tall:, :wide] = jnp.broadcast_to(upper[None], (peers, half, wide))
    out_ref[:, tall:, wide:] = jnp.broadcast_to(lower[None], (peers, half, wide))


def taper_slices(at, column_taper, row_taper, peers, parts):
    tall, wide = (column_taper.shape[0], column_taper.shape[1] // parts)
    rows, narrow = (row_taper.shape[0], row_taper.shape[1] // parts)
    return pl.pallas_call(
        slices_kernel,
        out_shape=shaped((peers, tall + rows // 2, wide), BF),
        grid_spec=pltpu.PrefetchScalarGridSpec(
            num_scalar_prefetch=1,
            grid=(1,),
            in_specs=[
                pl.BlockSpec((tall, wide), lambda i, at: (0, at[0])),
                pl.BlockSpec((rows, narrow), lambda i, at: (0, at[0])),
            ],
            out_specs=pl.BlockSpec((peers, tall + rows // 2, wide), lambda i, at: (0, 0, 0)),
        ),
        compiler_params=room(6),
        name="taper_slices",
    )(at, in_hbm(column_taper), in_hbm(row_taper))


def row_part_kernel(tall, slices_ref, out_ref):
    half = slices_ref.shape[1] - tall
    wide = out_ref.shape[2]
    out_ref[:, :half, :] = slices_ref[:, tall:, :wide]
    out_ref[:, half:, :] = slices_ref[:, tall:, wide:]


def row_part(slices, tall, settled):
    peers, height, wide = slices.shape
    return pl.pallas_call(
        lambda a, *rest: row_part_kernel(tall, a, rest[-1]),
        out_shape=shaped((peers, 2 * (height - tall), wide // 2), BF),
        in_specs=[pl.BlockSpec(memory_space=pltpu.VMEM)]
        + [pl.BlockSpec(memory_space=pl.ANY)] * len(settled),
        compiler_params=room(4),
        name="row_part",
    )(slices, *settled)


def columns_kernel(tall, fields_ref, slices_ref, out_ref):
    units, levels, rows, wide = out_ref.shape
    taper = slices_ref[:, :tall, :].reshape(-1, slices_ref.shape[2])
    product = jnp.dot(fields_ref[...], taper, preferred_element_type=F32).astype(BF)
    for member in range(units // 2):
        for side in range(2):
            part = product[
                member * levels * rows : (member + 1) * levels * rows,
                side * wide : (side + 1) * wide,
            ]
            out_ref[member * 2 + side] = part.reshape(levels, rows, wide)


def columns_pass(fields, slices, tall, levels, rows, parts):
    count, depth = fields.shape
    peers, height, wide = slices.shape
    units = 2 * count // (levels * rows)
    return pl.pallas_call(
        lambda a, b, c: columns_kernel(tall, a, b, c),
        out_shape=shaped((units, levels, rows, wide // 2), BF),
        grid=(parts,),
        in_specs=[
            pl.BlockSpec((count // parts, depth), lambda i: (i, 0)),
            pl.BlockSpec((peers, height, wide), lambda i: (0, 0, 0)),
        ],
        out_specs=pl.BlockSpec((units // parts, levels, rows, wide // 2), lambda i: (i, 0, 0, 0)),
        compiler_params=room(14),
        name="columns_pass",
    )(in_hbm(fields), slices)


def rows_kernel(taper_ref, fields_ref, *refs):
    out_ref, whole_ref = refs[-2:]
    peers, levels, rows, wide = fields_ref.shape

    @pl.when(pl.program_id(0) == 0)
    def _():
        for level in range(levels):
            whole_ref[:, level * wide : (level + 1) * wide] = fields_ref[:, level].reshape(
                peers * rows, wide
            )

    taper = jnp.concatenate([taper_ref[i] for i in range(taper_ref.shape[0])], axis=1)
    product = jnp.dot(taper, whole_ref[...], preferred_element_type=F32).astype(BF)
    for level in range(levels):
        out_ref[:, level] = product[:, level * wide : (level + 1) * wide].reshape(-1, rows, wide)


def rows_pass(taper, fields, blocks, settled):
    peers, levels, rows, wide = fields.shape
    parts, height, narrow = taper.shape
    return pl.pallas_call(
        rows_kernel,
        out_shape=shaped((peers, levels, rows, wide), BF),
        grid=(blocks,),
        in_specs=[
            pl.BlockSpec((parts, height // blocks, narrow), lambda i: (0, i, 0)),
            pl.BlockSpec((peers, levels, rows, wide), lambda i: (0, 0, 0, 0)),
        ]
        + [pl.BlockSpec(memory_space=pl.ANY)] * len(settled),
        out_specs=pl.BlockSpec((peers // blocks, levels, rows, wide), lambda i: (i, 0, 0, 0)),
        scratch_shapes=[pltpu.VMEM((height, levels * wide), BF)],
        compiler_params=room(10),
        name="rows_pass",
    )(in_hbm(taper), fields, *settled)


def split_kernel(at_ref, fields_ref, *out_refs):
    wide = out_refs[0].shape[-1]
    for step, out_ref in enumerate(out_refs):
        start = pl.multiple_of((at_ref[0] ^ step) * wide, wide)
        out_ref[...] = fields_ref[:, :, :, :, pl.ds(start, wide)]


def split_columns(at, fields, parts):
    shape = (*fields.shape[:-1], fields.shape[-1] // parts)
    return pl.pallas_call(
        split_kernel,
        out_shape=[shaped(shape, BF)] * parts,
        in_specs=[
            pl.BlockSpec(memory_space=pltpu.SMEM),
            pl.BlockSpec(memory_space=pltpu.VMEM),
        ],
        out_specs=[pl.BlockSpec(memory_space=pltpu.VMEM)] * parts,
        compiler_params=room(8),
        name="split_columns",
    )(at, fields)


def weight_kernel(parts, at_ref, localized_ref, *refs):
    weights = refs[:parts]
    out_ref, whole_ref, first_ref, last_ref = refs[parts:]
    variables, members, levels = weights[0].shape[:3]
    wide = localized_ref.shape[-1]
    for level in range(levels):
        for side in range(2):
            lanes = slice(side * wide, (side + 1) * wide)
            sums = [None] * variables
            for step in range(parts):
                base = (at_ref[0] ^ step) * (2 * members)
                for member in range(members):
                    field = localized_ref[base + 2 * member + side, level].astype(F32)
                    for k in range(variables):
                        term = weights[step][k, member, level, :, lanes].astype(F32) * field
                        sums[k] = term if sums[k] is None else sums[k] + term
            for k in range(variables):
                out_ref[k, level, :, lanes] = sums[k]
                rounded = sums[k].astype(BF)
                whole_ref[k, level, :, lanes] = rounded
                (first_ref, last_ref)[side][k, level] = rounded


def weighted_sum(at, localized, weights):
    variables, _, levels, rows, wide = weights[0].shape
    shape = (variables, levels, rows, wide)
    edge = (variables, levels, rows, wide // 2)
    vmem = pl.BlockSpec(memory_space=pltpu.VMEM)
    return pl.pallas_call(
        lambda *refs: weight_kernel(len(weights), *refs),
        out_shape=[shaped(shape, F32), shaped(shape, BF), shaped(edge, BF), shaped(edge, BF)],
        in_specs=[pl.BlockSpec(memory_space=pltpu.SMEM)] + [vmem] * (1 + len(weights)),
        out_specs=[vmem] * 4,
        compiler_params=room(8),
        name="weighted_sum",
    )(at, localized, *weights)


def beside(from_left, from_right):
    lane = lax.broadcasted_iota(jnp.int32, from_left.shape, from_left.ndim - 1)
    wide = from_left.shape[-1]
    none = jnp.zeros_like(from_left)
    kept = jnp.where(lane >= wide - STEPS, from_left, none)
    return jnp.where(lane < STEPS, from_right, kept)


def above_below(from_next, from_previous):
    row = lax.broadcasted_iota(jnp.int32, from_next.shape, from_next.ndim - 2)
    return jnp.where(row < STEPS, from_next, from_previous)


def widen_kernel(body_ref, left_ref, right_ref, out_ref):
    variables, levels, rows, wide = body_ref.shape
    for k in range(variables):
        for level in range(levels):
            out_ref[k, level, :, :wide] = body_ref[k, level]
            sides = beside(left_ref[k, level].astype(F32), right_ref[k, level].astype(F32))
            out_ref[k, level, :, wide:] = sides.astype(BF)


def widened(body, left, right):
    shape = (*body.shape[:-1], body.shape[-1] + left.shape[-1])
    return pl.pallas_call(
        widen_kernel,
        out_shape=shaped(shape, BF),
        compiler_params=room(4),
        name="widened",
    )(body, left, right)


def strips_kernel(own_ref, other_ref, top_ref, bottom_ref):
    variables, levels, rows, wide = own_ref.shape
    for rows_at, out_ref in ((slice(0, 8), top_ref), (slice(rows - 8, rows), bottom_ref)):
        for k in range(variables):
            for level in range(levels):
                out_ref[k, level] = own_ref[k, level, rows_at]
                out_ref[k, levels + level] = other_ref[k, level, rows_at]


def row_strips(own, other):
    variables, levels, rows, wide = own.shape
    return pl.pallas_call(
        strips_kernel,
        out_shape=[shaped((variables, 2 * levels, 8, wide), BF)] * 2,
        compiler_params=room(4),
        name="row_strips",
    )(own, other)


def advect_kernel(*refs):
    (
        flip_ref,
        own_ref,
        wider_ref,
        other_ref,
        next_ref,
        previous_ref,
        courant_ref,
        slope_ref,
        beside_ref,
        around_ref,
        opposite_ref,
        out_ref,
        first_ref,
        second_ref,
        terms_ref,
    ) = refs
    variables, levels, rows, wide = own_ref.shape
    deep, tall, full = first_ref.shape[1:]
    flip = flip_ref[0]
    sign = (1 - 2 * flip).astype(F32)
    directions = courant_ref.shape[0]

    def local(level):
        return jnp.where(flip == 1, levels - 1 - level, level)

    for level in range(deep):
        at = local(level % levels)
        mine = level < levels
        for k in range(variables):
            if mine:
                first_ref[k, level, :rows, :wide] = own_ref[k, at]
                first_ref[k, level, :rows, wide:] = wider_ref[k, at, :, wide:].astype(F32)
            else:
                first_ref[k, level, :rows, :] = other_ref[k, at].astype(F32)
            strip = at if mine else at + levels
            first_ref[k, level, rows:, :] = above_below(
                next_ref[k, strip].astype(F32), previous_ref[k, strip].astype(F32)
            )
        planes = []
        for a in range(directions + slope_ref.shape[0]):
            if mine:
                body = courant_ref[a, at] if a < directions else slope_ref[a - directions, at]
                upper = jnp.concatenate([body, beside_ref[a, at].astype(F32)], axis=1)
                plane = jnp.concatenate([upper, around_ref[a, at].astype(F32)], axis=0)
            else:
                plane = opposite_ref[a, at].astype(F32)
            planes.append(plane)
        planes[0] = planes[0] * sign
        kept = 1.0 - sum(jnp.abs(c) for c in planes[:directions])
        terms_ref[0, level] = kept
        for a in range(directions):
            terms_ref[1 + 2 * a, level] = jnp.maximum(planes[a], 0.0)
            terms_ref[2 + 2 * a, level] = -jnp.minimum(planes[a], 0.0)
        for a in range(directions, len(planes)):
            terms_ref[1 + directions + a, level] = planes[a]

    old_ref, new_ref = (first_ref, second_ref)
    for step in range(STEPS):
        reached = min(deep, levels + STEPS - 1 - step)
        last = step == STEPS - 1
        for level in range(reached):
            states = [old_ref[k, level] for k in range(variables)]
            for k in range(variables):
                state = states[k]
                total = terms_ref[0, level] * state
                if level > 0:
                    total = total + terms_ref[1, level] * old_ref[k, level - 1]
                if level + 1 < deep:
                    total = total + terms_ref[2, level] * old_ref[k, level + 1]
                total = total + terms_ref[3, level] * pltpu.roll(state, 1, 0)
                total = total + terms_ref[4, level] * pltpu.roll(state, tall - 1, 0)
                total = total + terms_ref[5, level] * pltpu.roll(state, 1, 1)
                total = total + terms_ref[6, level] * pltpu.roll(state, full - 1, 1)
                if k == 2:
                    total = total - (states[0] * terms_ref[7, level] + states[1] * terms_ref[8, level])
                if last:
                    out_ref[k, local(level)] = total[:rows, :wide]
                else:
                    new_ref[k, level] = total
        old_ref, new_ref = (new_ref, old_ref)


def advect(flip, *arrays):
    variables, levels, rows, wide = arrays[0].shape
    tall, full = (rows + 8, arrays[2].shape[-1])
    vmem = pl.BlockSpec(memory_space=pltpu.VMEM)
    state = pltpu.VMEM((variables, 2 * levels, tall, full), F32)
    return pl.pallas_call(
        advect_kernel,
        out_shape=shaped((variables, levels, rows, wide), F32),
        in_specs=[pl.BlockSpec(memory_space=pltpu.SMEM)] + [vmem] * len(arrays),
        out_specs=vmem,
        scratch_shapes=[state, state, pltpu.VMEM((9, 2 * levels, tall, full), F32)],
        compiler_params=room(14),
        name="advect",
    )(flip, *arrays)


def chain(axis, step):
    size = lax.axis_size(axis)
    return [(i, i + step) for i in range(size) if 0 <= i + step < size]


def swap(axis):
    return [(0, 1), (1, 0)]


def neighbours(first, last, axis):
    from_left = lax.ppermute(last, axis, chain(axis, 1))
    from_right = lax.ppermute(first, axis, chain(axis, -1))
    return from_left, from_right


def background(courant_numbers, tracer_slope):
    whole = jnp.concatenate([courant_numbers, tracer_slope], axis=0).astype(BF)
    half = whole.shape[-1] // 2
    sides = beside(*neighbours(whole[..., :half], whole[..., half:], "mem"))
    wider = jnp.concatenate([whole, sides], axis=-1)
    from_previous, from_next = neighbours(wider[:, :, :8], wider[:, :, -8:], "row")
    around = above_below(from_next, from_previous)
    return sides, around, jnp.concatenate([wider, around], axis=2)


def on_device(
    control_fields, perturbations, column_taper, row_taper, courant_numbers, tracer_slope
):
    members, levels, rows, columns = control_fields.shape
    parts, peers = (lax.axis_size("mem"), lax.axis_size("row"))
    tall = column_taper.shape[0]
    at = lax.axis_index("mem").astype(jnp.int32).reshape(1)
    flip = lax.axis_index("lev").astype(jnp.int32).reshape(1)

    every = lax.all_gather(
        control_fields.reshape(members * levels * rows, columns), "mem", axis=0, tiled=True
    )
    slices = lax.all_to_all(
        taper_slices(at, column_taper, row_taper, peers, parts), "row", 0, 0, tiled=True
    )
    sides, around, taller = background(courant_numbers, tracer_slope)
    pieces = split_columns(at, perturbations, parts)
    weights = dict(enumerate(pieces))

    def exchange(steps):
        for step in steps:
            pairs = [(i, i ^ step) for i in range(parts)]
            weights[step] = lax.ppermute(weights[step], "mem", pairs)
        return [weights[step] for step in steps]

    def hold(steps, settled):
        for step, piece in zip(steps, after([weights[step] for step in steps], settled)):
            weights[step] = piece

    settled = [*exchange((1,)), taller]
    first_pass = columns_pass(every, slices, tall, levels, rows, 2)
    row_whole = lax.all_gather(row_part(slices, tall, settled), "mem", axis=0, tiled=False)
    row_whole = row_whole.reshape(parts, row_taper.shape[1], -1)
    hold((2, 3, 6, 7), [first_pass])
    arrived = lax.all_to_all(first_pass, "row", 0, 0, tiled=True)
    tapered = rows_pass(row_whole, arrived, 4, exchange((2, 3, 6, 7)))
    hold((4, 5), [tapered])
    (taller,) = after([taller], [tapered])
    localized = lax.all_to_all(tapered, "row", 0, 0, tiled=True)
    exchange((4, 5))
    opposite = lax.ppermute(taller, "lev", swap("lev"))
    weights = [weights[step] for step in range(parts)]
    own, rounded, first, last = weighted_sum(at, localized, weights)

    wider = widened(rounded, *neighbours(first, last, "mem"))
    other = lax.ppermute(wider, "lev", swap("lev"))
    from_previous, from_next = neighbours(*row_strips(wider, other), "row")
    return advect(
        flip,
        own,
        wider,
        other,
        from_next,
        from_previous,
        courant_numbers,
        tracer_slope,
        sides,
        around,
        opposite,
    )


def solution(mesh):
    grid = P(None, "lev", "row", "mem")
    placed = (
        P("mem", "lev", "row", None),
        P(None, "mem", "lev", "row", None),
        P("row", None),
        P("row", None),
        grid,
        grid,
    )
    return jax.shard_map(
        on_device, mesh=mesh, in_specs=placed, out_specs=grid, check_vma=False
    )
```

```python
import jax
import jax.numpy as jnp
from jax import lax
from jax.experimental import pallas as pl
from jax.experimental.pallas import tpu as pltpu
from jax.sharding import PartitionSpec as P

STEPS = 4
BF = jnp.bfloat16
F32 = jnp.float32


def room(mebibytes):
    return pltpu.CompilerParams(vmem_limit_bytes=mebibytes * 1024 * 1024)


def in_hbm(x):
    return pltpu.with_memory_space_constraint(x, pltpu.HBM)


def shaped(shape, dtype):
    return jax.ShapeDtypeStruct(shape, dtype)


def after(arrays, settled):
    count = len(arrays)
    anywhere = pl.BlockSpec(memory_space=pl.ANY)
    return pl.pallas_call(
        lambda *refs: None,
        out_shape=[shaped(x.shape, x.dtype) for x in arrays],
        in_specs=[anywhere] * (count + len(settled)),
        out_specs=[anywhere] * count,
        input_output_aliases={i: i for i in range(count)},
        name="after",
    )(*arrays, *settled)


def slices_kernel(_, column_ref, row_ref, out_ref):
    tall = column_ref.shape[0]
    half = row_ref.shape[0] // 2
    wide = row_ref.shape[1]
    peers = out_ref.shape[0]
    out_ref[:, :tall, :] = jnp.broadcast_to(column_ref[...][None], (peers, *column_ref.shape))
    upper, lower = (row_ref[:half, :], row_ref[half:, :])
    out_ref[:, tall:, :wide] = jnp.broadcast_to(upper[None], (peers, half, wide))
    out_ref[:, tall:, wide:] = jnp.broadcast_to(lower[None], (peers, half, wide))


def taper_slices(at, column_taper, row_taper, peers, parts):
    tall, wide = (column_taper.shape[0], column_taper.shape[1] // parts)
    rows, narrow = (row_taper.shape[0], row_taper.shape[1] // parts)
    return pl.pallas_call(
        slices_kernel,
        out_shape=shaped((peers, tall + rows // 2, wide), BF),
        grid_spec=pltpu.PrefetchScalarGridSpec(
            num_scalar_prefetch=1,
            grid=(1,),
            in_specs=[
                pl.BlockSpec((tall, wide), lambda i, at: (0, at[0])),
                pl.BlockSpec((rows, narrow), lambda i, at: (0, at[0])),
            ],
            out_specs=pl.BlockSpec((peers, tall + rows // 2, wide), lambda i, at: (0, 0, 0)),
        ),
        compiler_params=room(6),
        name="taper_slices",
    )(at, in_hbm(column_taper), in_hbm(row_taper))


def row_part_kernel(tall, slices_ref, out_ref):
    half = slices_ref.shape[1] - tall
    wide = out_ref.shape[2]
    out_ref[:, :half, :] = slices_ref[:, tall:, :wide]
    out_ref[:, half:, :] = slices_ref[:, tall:, wide:]


def row_part(slices, tall, settled):
    peers, height, wide = slices.shape
    return pl.pallas_call(
        lambda a, *rest: row_part_kernel(tall, a, rest[-1]),
        out_shape=shaped((peers, 2 * (height - tall), wide // 2), BF),
        in_specs=[pl.BlockSpec(memory_space=pltpu.VMEM)]
        + [pl.BlockSpec(memory_space=pl.ANY)] * len(settled),
        compiler_params=room(4),
        name="row_part",
    )(slices, *settled)


def columns_kernel(tall, fields_ref, slices_ref, out_ref):
    units, levels, rows, wide = out_ref.shape
    taper = slices_ref[:, :tall, :].reshape(-1, slices_ref.shape[2])
    product = jnp.dot(fields_ref[...], taper, preferred_element_type=F32).astype(BF)
    for member in range(units // 2):
        for side in range(2):
            part = product[
                member * levels * rows : (member + 1) * levels * rows,
                side * wide : (side + 1) * wide,
            ]
            out_ref[member * 2 + side] = part.reshape(levels, rows, wide)


def columns_pass(fields, slices, tall, levels, rows, parts):
    count, depth = fields.shape
    peers, height, wide = slices.shape
    units = 2 * count // (levels * rows)
    return pl.pallas_call(
        lambda a, b, c: columns_kernel(tall, a, b, c),
        out_shape=shaped((units, levels, rows, wide // 2), BF),
        grid=(parts,),
        in_specs=[
            pl.BlockSpec((count // parts, depth), lambda i: (i, 0)),
            pl.BlockSpec((peers, height, wide), lambda i: (0, 0, 0)),
        ],
        out_specs=pl.BlockSpec((units // parts, levels, rows, wide // 2), lambda i: (i, 0, 0, 0)),
        compiler_params=room(14),
        name="columns_pass",
    )(in_hbm(fields), slices)


def join_kernel(parts_ref, out_ref):
    for i in range(parts_ref.shape[0]):
        wide = parts_ref.shape[2]
        out_ref[:, i * wide : (i + 1) * wide] = parts_ref[i]


def joined(taper, blocks):
    parts, height, narrow = taper.shape
    return pl.pallas_call(
        join_kernel,
        out_shape=shaped((height, parts * narrow), BF),
        grid=(blocks,),
        in_specs=[pl.BlockSpec((parts, height // blocks, narrow), lambda i: (0, i, 0))],
        out_specs=pl.BlockSpec((height // blocks, parts * narrow), lambda i: (i, 0)),
        compiler_params=room(6),
        name="joined",
    )(in_hbm(taper))


def rows_kernel(taper_ref, fields_ref, *refs):
    out_ref, whole_ref = refs[-2:]
    peers, levels, rows, wide = fields_ref.shape
    for level in range(levels):
        whole_ref[:, level * wide : (level + 1) * wide] = fields_ref[:, level].reshape(
            peers * rows, wide
        )
    product = jnp.dot(taper_ref[...], whole_ref[...], preferred_element_type=F32).astype(BF)
    for level in range(levels):
        out_ref[:, level] = product[:, level * wide : (level + 1) * wide].reshape(-1, rows, wide)


def rows_pass(taper, fields, settled):
    peers, levels, rows, wide = fields.shape
    vmem = pl.BlockSpec(memory_space=pltpu.VMEM)
    return pl.pallas_call(
        rows_kernel,
        out_shape=shaped((peers, levels, rows, wide), BF),
        in_specs=[vmem, vmem] + [pl.BlockSpec(memory_space=pl.ANY)] * len(settled),
        out_specs=vmem,
        scratch_shapes=[pltpu.VMEM((peers * rows, levels * wide), BF)],
        compiler_params=room(12),
        name="rows_pass",
    )(taper, fields, *settled)


def split_kernel(at_ref, fields_ref, *out_refs):
    wide = out_refs[0].shape[-1]
    for step, out_ref in enumerate(out_refs):
        start = pl.multiple_of((at_ref[0] ^ step) * wide, wide)
        out_ref[...] = fields_ref[:, :, :, :, pl.ds(start, wide)]


def split_columns(at, fields, parts):
    shape = (*fields.shape[:-1], fields.shape[-1] // parts)
    return pl.pallas_call(
        split_kernel,
        out_shape=[shaped(shape, BF)] * parts,
        in_specs=[
            pl.BlockSpec(memory_space=pltpu.SMEM),
            pl.BlockSpec(memory_space=pltpu.VMEM),
        ],
        out_specs=[pl.BlockSpec(memory_space=pltpu.VMEM)] * parts,
        compiler_params=room(8),
        name="split_columns",
    )(at, fields)


def weight_kernel(parts, at_ref, localized_ref, *refs):
    weights = refs[:parts]
    out_ref, whole_ref, first_ref, last_ref = refs[parts:]
    variables, members, levels = weights[0].shape[:3]
    wide = localized_ref.shape[-1]
    for level in range(levels):
        for side in range(2):
            lanes = slice(side * wide, (side + 1) * wide)
            sums = [None] * variables
            for step in range(parts):
                base = (at_ref[0] ^ step) * (2 * members)
                for member in range(members):
                    field = localized_ref[base + 2 * member + side, level].astype(F32)
                    for k in range(variables):
                        term = weights[step][k, member, level, :, lanes].astype(F32) * field
                        sums[k] = term if sums[k] is None else sums[k] + term
            for k in range(variables):
                out_ref[k, level, :, lanes] = sums[k]
                rounded = sums[k].astype(BF)
                whole_ref[k, level, :, lanes] = rounded
                (first_ref, last_ref)[side][k, level] = rounded


def weighted_sum(at, localized, weights):
    variables, _, levels, rows, wide = weights[0].shape
    shape = (variables, levels, rows, wide)
    edge = (variables, levels, rows, wide // 2)
    vmem = pl.BlockSpec(memory_space=pltpu.VMEM)
    return pl.pallas_call(
        lambda *refs: weight_kernel(len(weights), *refs),
        out_shape=[shaped(shape, F32), shaped(shape, BF), shaped(edge, BF), shaped(edge, BF)],
        in_specs=[pl.BlockSpec(memory_space=pltpu.SMEM)] + [vmem] * (1 + len(weights)),
        out_specs=[vmem] * 4,
        compiler_params=room(8),
        name="weighted_sum",
    )(at, localized, *weights)


def beside(from_left, from_right):
    lane = lax.broadcasted_iota(jnp.int32, from_left.shape, from_left.ndim - 1)
    wide = from_left.shape[-1]
    none = jnp.zeros_like(from_left)
    kept = jnp.where(lane >= wide - STEPS, from_left, none)
    return jnp.where(lane < STEPS, from_right, kept)


def above_below(from_next, from_previous):
    row = lax.broadcasted_iota(jnp.int32, from_next.shape, from_next.ndim - 2)
    return jnp.where(row < STEPS, from_next, from_previous)


def widen_kernel(body_ref, left_ref, right_ref, out_ref, top_ref, bottom_ref):
    variables, levels, rows, wide = body_ref.shape
    for k in range(variables):
        for level in range(levels):
            out_ref[k, level, :, :wide] = body_ref[k, level]
            sides = beside(left_ref[k, level].astype(F32), right_ref[k, level].astype(F32))
            out_ref[k, level, :, wide:] = sides.astype(BF)
            top_ref[k, level] = out_ref[k, level, :8]
            bottom_ref[k, level] = out_ref[k, level, rows - 8 :]


def widened(body, left, right):
    variables, levels, rows, wide = body.shape
    full = wide + left.shape[-1]
    strip = shaped((variables, levels, 8, full), BF)
    return pl.pallas_call(
        widen_kernel,
        out_shape=[shaped((variables, levels, rows, full), BF), strip, strip],
        compiler_params=room(4),
        name="widened",
    )(body, left, right)


def ring_kernel(next_ref, previous_ref, out_ref):
    for k in range(out_ref.shape[0]):
        for level in range(out_ref.shape[1]):
            rows = above_below(
                next_ref[k, level].astype(F32), previous_ref[k, level].astype(F32)
            )
            out_ref[k, level] = rows.astype(BF)


def ring(from_next, from_previous):
    return pl.pallas_call(
        ring_kernel,
        out_shape=shaped(from_next.shape, BF),
        compiler_params=room(4),
        name="ring",
    )(from_next, from_previous)


def advect_kernel(*refs):
    (
        flip_ref,
        own_ref,
        wider_ref,
        other_ref,
        ring_ref,
        other_ring_ref,
        courant_ref,
        slope_ref,
        beside_ref,
        around_ref,
        opposite_ref,
        out_ref,
        first_ref,
        second_ref,
        terms_ref,
        held_ref,
        arrival,
    ) = refs
    fetch = pltpu.make_async_copy(own_ref, held_ref, arrival)
    fetch.start()
    variables, levels, rows, wide = own_ref.shape
    deep, tall, full = first_ref.shape[1:]
    flip = flip_ref[0]
    sign = (1 - 2 * flip).astype(F32)
    directions = courant_ref.shape[0]

    def local(level):
        return jnp.where(flip == 1, levels - 1 - level, level)

    for level in range(deep):
        at = local(level % levels)
        mine = level < levels
        for k in range(variables):
            if mine:
                first_ref[k, level, :rows, wide:] = wider_ref[k, at, :, wide:].astype(F32)
            else:
                first_ref[k, level, :rows, :] = other_ref[k, at].astype(F32)
            strip_ref = ring_ref if mine else other_ring_ref
            first_ref[k, level, rows:, :] = strip_ref[k, at].astype(F32)
        planes = []
        for a in range(directions + slope_ref.shape[0]):
            if mine:
                body = courant_ref[a, at] if a < directions else slope_ref[a - directions, at]
                upper = jnp.concatenate([body, beside_ref[a, at].astype(F32)], axis=1)
                plane = jnp.concatenate([upper, around_ref[a, at].astype(F32)], axis=0)
            else:
                plane = opposite_ref[a, at].astype(F32)
            planes.append(plane)
        planes[0] = planes[0] * sign
        kept = 1.0 - sum(jnp.abs(c) for c in planes[:directions])
        terms_ref[0, level] = kept
        for a in range(directions):
            terms_ref[1 + 2 * a, level] = jnp.maximum(planes[a], 0.0)
            terms_ref[2 + 2 * a, level] = -jnp.minimum(planes[a], 0.0)
        for a in range(directions, len(planes)):
            terms_ref[1 + directions + a, level] = planes[a]

    fetch.wait()
    for level in range(levels):
        for k in range(variables):
            first_ref[k, level, :rows, :wide] = held_ref[k, local(level)]

    old_ref, new_ref = (first_ref, second_ref)
    for step in range(STEPS):
        reached = min(deep, levels + STEPS - 1 - step)
        last = step == STEPS - 1
        for level in range(reached):
            states = [old_ref[k, level] for k in range(variables)]
            for k in range(variables):
                state = states[k]
                total = terms_ref[0, level] * state
                if level > 0:
                    total = total + terms_ref[1, level] * old_ref[k, level - 1]
                if level + 1 < deep:
                    total = total + terms_ref[2, level] * old_ref[k, level + 1]
                total = total + terms_ref[3, level] * pltpu.roll(state, 1, 0)
                total = total + terms_ref[4, level] * pltpu.roll(state, tall - 1, 0)
                total = total + terms_ref[5, level] * pltpu.roll(state, 1, 1)
                total = total + terms_ref[6, level] * pltpu.roll(state, full - 1, 1)
                if k == 2:
                    total = total - (states[0] * terms_ref[7, level] + states[1] * terms_ref[8, level])
                if last:
                    out_ref[k, local(level)] = total[:rows, :wide]
                else:
                    new_ref[k, level] = total
        old_ref, new_ref = (new_ref, old_ref)


def advect(flip, *arrays):
    variables, levels, rows, wide = arrays[0].shape
    tall, full = (rows + 8, arrays[2].shape[-1])
    vmem = pl.BlockSpec(memory_space=pltpu.VMEM)
    state = pltpu.VMEM((variables, 2 * levels, tall, full), F32)
    return pl.pallas_call(
        advect_kernel,
        out_shape=shaped((variables, levels, rows, wide), F32),
        in_specs=[pl.BlockSpec(memory_space=pltpu.SMEM), pl.BlockSpec(memory_space=pl.ANY)]
        + [vmem] * (len(arrays) - 1),
        out_specs=vmem,
        scratch_shapes=[
            state,
            state,
            pltpu.VMEM((9, 2 * levels, tall, full), F32),
            pltpu.VMEM((variables, levels, rows, wide), F32),
            pltpu.SemaphoreType.DMA(()),
        ],
        compiler_params=room(14),
        name="advect",
    )(flip, *arrays)


def chain(axis, step):
    size = lax.axis_size(axis)
    return [(i, i + step) for i in range(size) if 0 <= i + step < size]


def swap(axis):
    return [(0, 1), (1, 0)]


def neighbours(first, last, axis):
    from_left = lax.ppermute(last, axis, chain(axis, 1))
    from_right = lax.ppermute(first, axis, chain(axis, -1))
    return from_left, from_right


def background(courant_numbers, tracer_slope):
    whole = jnp.concatenate([courant_numbers, tracer_slope], axis=0).astype(BF)
    half = whole.shape[-1] // 2
    sides = beside(*neighbours(whole[..., :half], whole[..., half:], "mem"))
    wider = jnp.concatenate([whole, sides], axis=-1)
    from_previous, from_next = neighbours(wider[:, :, :8], wider[:, :, -8:], "row")
    around = above_below(from_next, from_previous)
    return sides, around, jnp.concatenate([wider, around], axis=2)


def on_device(
    control_fields, perturbations, column_taper, row_taper, courant_numbers, tracer_slope
):
    members, levels, rows, columns = control_fields.shape
    parts, peers = (lax.axis_size("mem"), lax.axis_size("row"))
    tall = column_taper.shape[0]
    at = lax.axis_index("mem").astype(jnp.int32).reshape(1)
    flip = lax.axis_index("lev").astype(jnp.int32).reshape(1)

    every = lax.all_gather(
        control_fields.reshape(members * levels * rows, columns), "mem", axis=0, tiled=True
    )
    slices = lax.all_to_all(
        taper_slices(at, column_taper, row_taper, peers, parts), "row", 0, 0, tiled=True
    )
    sides, around, taller = background(courant_numbers, tracer_slope)
    pieces = split_columns(at, perturbations, parts)
    weights = dict(enumerate(pieces))

    def exchange(steps):
        for step in steps:
            pairs = [(i, i ^ step) for i in range(parts)]
            weights[step] = lax.ppermute(weights[step], "mem", pairs)
        return [weights[step] for step in steps]

    def hold(steps, settled):
        for step, piece in zip(steps, after([weights[step] for step in steps], settled)):
            weights[step] = piece

    settled = [*exchange((1,)), taller]
    (taller,) = after([taller], [slices])
    opposite = lax.ppermute(taller, "lev", swap("lev"))
    first_pass = columns_pass(every, slices, tall, levels, rows, 2)
    row_whole = lax.all_gather(row_part(slices, tall, settled), "mem", axis=0, tiled=False)
    row_whole = row_whole.reshape(parts, row_taper.shape[1], -1)
    hold((2, 3, 6, 7), [first_pass])
    arrived = lax.all_to_all(first_pass, "row", 0, 0, tiled=True)
    tapered = rows_pass(joined(row_whole, 4), arrived, [*exchange((2, 3, 6, 7)), opposite])
    hold((4, 5), [tapered])
    localized = lax.all_to_all(tapered, "row", 0, 0, tiled=True)
    exchange((4, 5))
    weights = [weights[step] for step in range(parts)]
    own, rounded, first, last = weighted_sum(at, localized, weights)

    wider, top, bottom = widened(rounded, *neighbours(first, last, "mem"))
    other = lax.ppermute(wider, "lev", swap("lev"))
    from_previous, from_next = neighbours(top, bottom, "row")
    rows_around = ring(from_next, from_previous)
    return advect(
        flip,
        own,
        wider,
        other,
        rows_around,
        lax.ppermute(rows_around, "lev", swap("lev")),
        courant_numbers,
        tracer_slope,
        sides,
        around,
        opposite,
    )


def solution(mesh):
    grid = P(None, "lev", "row", "mem")
    placed = (
        P("mem", "lev", "row", None),
        P(None, "mem", "lev", "row", None),
        P("row", None),
        P("row", None),
        grid,
        grid,
    )
    return jax.shard_map(
        on_device, mesh=mesh, in_specs=placed, out_specs=grid, check_vma=False
    )
```

```python
import jax
import jax.numpy as jnp
from jax import lax
from jax.experimental import pallas as pl
from jax.experimental.pallas import tpu as pltpu
from jax.sharding import PartitionSpec as P

STEPS = 4
BF = jnp.bfloat16
F32 = jnp.float32


def room(mebibytes):
    return pltpu.CompilerParams(vmem_limit_bytes=mebibytes * 1024 * 1024)


def in_hbm(x):
    return pltpu.with_memory_space_constraint(x, pltpu.HBM)


def shaped(shape, dtype):
    return jax.ShapeDtypeStruct(shape, dtype)


def after(arrays, settled):
    count = len(arrays)
    anywhere = pl.BlockSpec(memory_space=pl.ANY)
    return pl.pallas_call(
        lambda *refs: None,
        out_shape=[shaped(x.shape, x.dtype) for x in arrays],
        in_specs=[anywhere] * (count + len(settled)),
        out_specs=[anywhere] * count,
        input_output_aliases={i: i for i in range(count)},
        name="after",
    )(*arrays, *settled)


def slices_kernel(which_ref, column_ref, row_ref, out_ref):
    peers, height, wide = out_ref.shape
    tall = column_ref.shape[0]
    narrow = row_ref.shape[1] // 2
    out_ref[:, :tall, :] = jnp.broadcast_to(column_ref[...][None], (peers, *column_ref.shape))
    mine = row_ref[...].astype(F32)
    mine = jnp.where(which_ref[1] == 1, mine[:, narrow:], mine[:, :narrow]).astype(BF)
    pieces = [mine[8 * i : 8 * i + 8] for i in range(wide // narrow)]
    slab = jnp.concatenate(pieces, axis=1)
    out_ref[:, tall:, :] = jnp.broadcast_to(slab[None], (peers, *slab.shape))


def taper_slices(which, column_taper, row_taper, peers, parts):
    tall, wide = (column_taper.shape[0], column_taper.shape[1] // parts)
    rows, narrow = (row_taper.shape[0], row_taper.shape[1] // parts)
    shape = (peers, tall + rows * narrow // 2 // wide, wide)
    return pl.pallas_call(
        slices_kernel,
        out_shape=shaped(shape, BF),
        grid_spec=pltpu.PrefetchScalarGridSpec(
            num_scalar_prefetch=1,
            grid=(1,),
            in_specs=[
                pl.BlockSpec((tall, wide), lambda i, which: (0, which[0])),
                pl.BlockSpec((rows, narrow), lambda i, which: (0, which[0])),
            ],
            out_specs=pl.BlockSpec(shape, lambda i, which: (0, 0, 0)),
        ),
        compiler_params=room(6),
        name="taper_slices",
    )(which, in_hbm(column_taper), in_hbm(row_taper))


def row_part(slices, tall, settled):
    peers, height, wide = slices.shape

    def kernel(slices_ref, *refs):
        refs[-1][...] = slices_ref[:, tall:, :]

    return pl.pallas_call(
        kernel,
        out_shape=shaped((peers, height - tall, wide), BF),
        in_specs=[pl.BlockSpec(memory_space=pltpu.VMEM)]
        + [pl.BlockSpec(memory_space=pl.ANY)] * len(settled),
        compiler_params=room(4),
        name="row_part",
    )(slices, *settled)


def columns_kernel(tall, *refs):
    slices_ref, out_ref = refs[-2:]
    units, levels, rows, wide = out_ref.shape
    product = None
    for i, fields_ref in enumerate(refs[:-2]):
        depth = fields_ref.shape[1]
        count = depth // tall
        taper = slices_ref[i * count : (i + 1) * count, :tall, :].reshape(depth, 2 * wide)
        part = jnp.dot(fields_ref[...], taper, preferred_element_type=F32)
        product = part if product is None else product + part
    product = product.astype(BF)
    for member in range(units // 2):
        for side in range(2):
            part = product[
                member * levels * rows : (member + 1) * levels * rows,
                side * wide : (side + 1) * wide,
            ]
            out_ref[member * 2 + side] = part.reshape(levels, rows, wide)


def columns_pass(fields, slices, tall, levels, rows, blocks, streams):
    count, depth = fields.shape
    peers, height, wide = slices.shape
    units = 2 * count // (levels * rows)
    fields = in_hbm(fields)

    def stream(j):
        return pl.BlockSpec((count // blocks, depth // streams), lambda i: (i, j))

    return pl.pallas_call(
        lambda *refs: columns_kernel(tall, *refs),
        out_shape=shaped((units, levels, rows, wide // 2), BF),
        grid=(blocks,),
        in_specs=[stream(j) for j in range(streams)]
        + [pl.BlockSpec((peers, height, wide), lambda i: (0, 0, 0))],
        out_specs=pl.BlockSpec((units // blocks, levels, rows, wide // 2), lambda i: (i, 0, 0, 0)),
        compiler_params=room(14),
        name="columns_pass",
    )(*[fields] * streams, slices)


def pair_kernel(own_ref, other_ref, _, out_ref):
    out_ref[0] = own_ref[...]
    out_ref[1] = other_ref[...]


def paired(own, other, settled):
    whole = pl.BlockSpec(own.shape, lambda i: (0, 0, 0))
    return pl.pallas_call(
        pair_kernel,
        out_shape=shaped((2, *own.shape), own.dtype),
        grid=(1,),
        in_specs=[whole, whole, pl.BlockSpec(memory_space=pl.ANY)],
        out_specs=pl.BlockSpec((2, *own.shape), lambda i: (0, 0, 0, 0)),
        compiler_params=room(4),
        name="paired",
    )(own, other, settled)


def join_kernel(flip_ref, parts_ref, out_ref):
    parts, _, count, tall, wide = parts_ref.shape
    pieces = out_ref.shape[1] // tall
    narrow = wide // pieces
    for part in range(parts):
        for j in range(count):
            pair = [parts_ref[part, k ^ flip_ref[0], j].astype(F32) for k in range(2)]
            for i in range(pieces):
                lanes = slice(i * narrow, (i + 1) * narrow)
                both = jnp.concatenate([x[:, lanes] for x in pair], axis=1)
                at = slice(part * 2 * narrow, (part + 1) * 2 * narrow)
                out_ref[j, i * tall : (i + 1) * tall, at] = both.astype(BF)


def joined(flip, taper, rows, blocks):
    parts, _, peers, tall, wide = taper.shape
    across = 2 * parts * tall * wide // rows
    count = peers // blocks
    whole = pl.pallas_call(
        join_kernel,
        out_shape=shaped((peers, rows, across), BF),
        grid_spec=pltpu.PrefetchScalarGridSpec(
            num_scalar_prefetch=1,
            grid=(blocks,),
            in_specs=[
                pl.BlockSpec((parts, 2, count, tall, wide), lambda i, flip: (0, 0, i, 0, 0))
            ],
            out_specs=pl.BlockSpec((count, rows, across), lambda i, flip: (i, 0, 0)),
        ),
        compiler_params=room(6),
        name="joined",
    )(flip, in_hbm(taper))
    return whole.reshape(peers * rows, across)


def rows_kernel(taper_ref, fields_ref, *refs):
    out_ref, whole_ref = refs[-2:]
    peers, levels, rows, wide = fields_ref.shape
    for level in range(levels):
        whole_ref[:, level * wide : (level + 1) * wide] = fields_ref[:, level].reshape(
            peers * rows, wide
        )
    product = jnp.dot(taper_ref[...], whole_ref[...], preferred_element_type=F32).astype(BF)
    for level in range(levels):
        out_ref[:, level] = product[:, level * wide : (level + 1) * wide].reshape(-1, rows, wide)


def rows_pass(taper, fields, settled):
    peers, levels, rows, wide = fields.shape
    vmem = pl.BlockSpec(memory_space=pltpu.VMEM)
    return pl.pallas_call(
        rows_kernel,
        out_shape=shaped((peers, levels, rows, wide), BF),
        in_specs=[vmem, vmem] + [pl.BlockSpec(memory_space=pl.ANY)] * len(settled),
        out_specs=vmem,
        scratch_shapes=[pltpu.VMEM((peers * rows, levels * wide), BF)],
        compiler_params=room(12),
        name="rows_pass",
    )(taper, fields, *settled)


def split_kernel(at_ref, fields_ref, *out_refs):
    wide = out_refs[0].shape[-1]
    for step, out_ref in enumerate(out_refs):
        start = pl.multiple_of((at_ref[0] ^ step) * wide, wide)
        out_ref[...] = fields_ref[:, :, :, :, pl.ds(start, wide)]


def split_columns(at, fields, parts):
    shape = (*fields.shape[:-1], fields.shape[-1] // parts)
    return pl.pallas_call(
        split_kernel,
        out_shape=[shaped(shape, BF)] * parts,
        in_specs=[
            pl.BlockSpec(memory_space=pltpu.SMEM),
            pl.BlockSpec(memory_space=pltpu.VMEM),
        ],
        out_specs=[pl.BlockSpec(memory_space=pltpu.VMEM)] * parts,
        compiler_params=room(8),
        name="split_columns",
    )(at, fields)


def weight_kernel(parts, at_ref, localized_ref, *refs):
    weights = refs[:parts]
    out_ref, whole_ref, first_ref, last_ref = refs[parts:]
    variables, members, levels = weights[0].shape[:3]
    wide = localized_ref.shape[-1]
    for level in range(levels):
        for side in range(2):
            lanes = slice(side * wide, (side + 1) * wide)
            sums = [None] * variables
            for step in range(parts):
                base = (at_ref[0] ^ step) * (2 * members)
                for member in range(members):
                    field = localized_ref[base + 2 * member + side, level].astype(F32)
                    for k in range(variables):
                        term = weights[step][k, member, level, :, lanes].astype(F32) * field
                        sums[k] = term if sums[k] is None else sums[k] + term
            for k in range(variables):
                out_ref[k, level, :, lanes] = sums[k]
                rounded = sums[k].astype(BF)
                whole_ref[k, level, :, lanes] = rounded
                (first_ref, last_ref)[side][k, level] = rounded


def weighted_sum(at, localized, weights):
    variables, _, levels, rows, wide = weights[0].shape
    shape = (variables, levels, rows, wide)
    edge = (variables, levels, rows, wide // 2)
    vmem = pl.BlockSpec(memory_space=pltpu.VMEM)
    return pl.pallas_call(
        lambda *refs: weight_kernel(len(weights), *refs),
        out_shape=[shaped(shape, F32), shaped(shape, BF), shaped(edge, BF), shaped(edge, BF)],
        in_specs=[pl.BlockSpec(memory_space=pltpu.SMEM)] + [vmem] * (1 + len(weights)),
        out_specs=[vmem] * 4,
        compiler_params=room(8),
        name="weighted_sum",
    )(at, localized, *weights)


def beside(from_left, from_right):
    lane = lax.broadcasted_iota(jnp.int32, from_left.shape, from_left.ndim - 1)
    wide = from_left.shape[-1]
    none = jnp.zeros_like(from_left)
    kept = jnp.where(lane >= wide - STEPS, from_left, none)
    return jnp.where(lane < STEPS, from_right, kept)


def above_below(from_next, from_previous):
    row = lax.broadcasted_iota(jnp.int32, from_next.shape, from_next.ndim - 2)
    return jnp.where(row < STEPS, from_next, from_previous)


def edges_kernel(body_ref, left_ref, right_ref, sides_ref, top_ref, bottom_ref):
    variables, levels, rows, wide = body_ref.shape
    for k in range(variables):
        for level in range(levels):
            sides = beside(left_ref[k, level].astype(F32), right_ref[k, level].astype(F32))
            sides_ref[k, level] = sides.astype(BF)
            for at, out_ref in ((slice(0, 8), top_ref), (slice(rows - 8, rows), bottom_ref)):
                out_ref[k, level, :, :wide] = body_ref[k, level, at]
                out_ref[k, level, :, wide:] = sides_ref[k, level, at]


def edges(body, left, right):
    variables, levels, rows, wide = body.shape
    strip = shaped((variables, levels, 8, wide + left.shape[-1]), BF)
    return pl.pallas_call(
        edges_kernel,
        out_shape=[shaped(left.shape, BF), strip, strip],
        compiler_params=room(4),
        name="edges",
    )(body, left, right)


def frame_kernel(sides_ref, next_ref, previous_ref, out_ref):
    variables, levels, rows, wide = sides_ref.shape
    for k in range(variables):
        for level in range(levels):
            out_ref[k, level, :rows] = sides_ref[k, level]
            around = above_below(
                next_ref[k, level].astype(F32), previous_ref[k, level].astype(F32)
            ).astype(BF)
            for i in range(around.shape[1] // wide):
                at = rows + 8 * i
                out_ref[k, level, at : at + 8] = around[:, i * wide : (i + 1) * wide]


def frame(sides, from_next, from_previous):
    variables, levels, rows, wide = sides.shape
    tall = rows + 8 * (from_next.shape[-1] // wide)
    return pl.pallas_call(
        frame_kernel,
        out_shape=shaped((variables, levels, tall, wide), BF),
        compiler_params=room(4),
        name="frame",
    )(sides, from_next, from_previous)


def advect_kernel(*refs):
    (
        flip_ref,
        own_ref,
        other_ref,
        frame_ref,
        other_frame_ref,
        courant_ref,
        slope_ref,
        beside_ref,
        around_ref,
        opposite_ref,
        out_ref,
        first_ref,
        second_ref,
        terms_ref,
        held_ref,
        arrival,
    ) = refs
    fetch = pltpu.make_async_copy(own_ref, held_ref, arrival)
    fetch.start()
    variables, levels, rows, wide = own_ref.shape
    deep, tall, full = first_ref.shape[1:]
    flip = flip_ref[0]
    sign = (1 - 2 * flip).astype(F32)
    directions = courant_ref.shape[0]

    def local(level):
        return jnp.where(flip == 1, levels - 1 - level, level)

    for level in range(deep):
        at = local(level % levels)
        mine = level < levels
        for k in range(variables):
            around_of = frame_ref if mine else other_frame_ref
            if not mine:
                first_ref[k, level, :rows, :wide] = other_ref[k, at].astype(F32)
            first_ref[k, level, :rows, wide:] = around_of[k, at, :rows].astype(F32)
            for i in range(full // (full - wide)):
                lanes = slice(i * (full - wide), (i + 1) * (full - wide))
                strip = around_of[k, at, rows + 8 * i : rows + 8 * (i + 1)]
                first_ref[k, level, rows:, lanes] = strip.astype(F32)
        planes = []
        for a in range(directions + slope_ref.shape[0]):
            if mine:
                body = courant_ref[a, at] if a < directions else slope_ref[a - directions, at]
                upper = jnp.concatenate([body, beside_ref[a, at].astype(F32)], axis=1)
                plane = jnp.concatenate([upper, around_ref[a, at].astype(F32)], axis=0)
            else:
                plane = opposite_ref[a, at].astype(F32)
            planes.append(plane)
        planes[0] = planes[0] * sign
        kept = 1.0 - sum(jnp.abs(c) for c in planes[:directions])
        terms_ref[0, level] = kept
        for a in range(directions):
            terms_ref[1 + 2 * a, level] = jnp.maximum(planes[a], 0.0)
            terms_ref[2 + 2 * a, level] = -jnp.minimum(planes[a], 0.0)
        for a in range(directions, len(planes)):
            terms_ref[1 + directions + a, level] = planes[a]

    fetch.wait()
    for level in range(levels):
        for k in range(variables):
            first_ref[k, level, :rows, :wide] = held_ref[k, local(level)]

    old_ref, new_ref = (first_ref, second_ref)
    for step in range(STEPS):
        reached = min(deep, levels + STEPS - 1 - step)
        last = step == STEPS - 1
        for level in range(reached):
            states = [old_ref[k, level] for k in range(variables)]
            for k in range(variables):
                state = states[k]
                total = terms_ref[0, level] * state
                if level > 0:
                    total = total + terms_ref[1, level] * old_ref[k, level - 1]
                if level + 1 < deep:
                    total = total + terms_ref[2, level] * old_ref[k, level + 1]
                total = total + terms_ref[3, level] * pltpu.roll(state, 1, 0)
                total = total + terms_ref[4, level] * pltpu.roll(state, tall - 1, 0)
                total = total + terms_ref[5, level] * pltpu.roll(state, 1, 1)
                total = total + terms_ref[6, level] * pltpu.roll(state, full - 1, 1)
                if k == 2:
                    total = total - (states[0] * terms_ref[7, level] + states[1] * terms_ref[8, level])
                if last:
                    out_ref[k, local(level)] = total[:rows, :wide]
                else:
                    new_ref[k, level] = total
        old_ref, new_ref = (new_ref, old_ref)


def advect(flip, *arrays):
    variables, levels, rows, wide = arrays[0].shape
    tall, full = (rows + 8, wide + arrays[2].shape[-1])
    vmem = pl.BlockSpec(memory_space=pltpu.VMEM)
    state = pltpu.VMEM((variables, 2 * levels, tall, full), F32)
    return pl.pallas_call(
        advect_kernel,
        out_shape=shaped((variables, levels, rows, wide), F32),
        in_specs=[pl.BlockSpec(memory_space=pltpu.SMEM), pl.BlockSpec(memory_space=pl.ANY)]
        + [vmem] * (len(arrays) - 1),
        out_specs=vmem,
        scratch_shapes=[
            state,
            state,
            pltpu.VMEM((9, 2 * levels, tall, full), F32),
            pltpu.VMEM((variables, levels, rows, wide), F32),
            pltpu.SemaphoreType.DMA(()),
        ],
        compiler_params=room(14),
        name="advect",
    )(flip, *arrays)


def chain(axis, step):
    size = lax.axis_size(axis)
    return [(i, i + step) for i in range(size) if 0 <= i + step < size]


def swap(axis):
    return [(0, 1), (1, 0)]


def neighbours(first, last, axis):
    from_left = lax.ppermute(last, axis, chain(axis, 1))
    from_right = lax.ppermute(first, axis, chain(axis, -1))
    return from_left, from_right


def background(courant_numbers, tracer_slope):
    whole = jnp.concatenate([courant_numbers, tracer_slope], axis=0).astype(BF)
    half = whole.shape[-1] // 2
    sides = beside(*neighbours(whole[..., :half], whole[..., half:], "mem"))
    wider = jnp.concatenate([whole, sides], axis=-1)
    from_previous, from_next = neighbours(wider[:, :, :8], wider[:, :, -8:], "row")
    around = above_below(from_next, from_previous)
    return sides, around, jnp.concatenate([wider, around], axis=2)


def on_device(
    control_fields, perturbations, column_taper, row_taper, courant_numbers, tracer_slope
):
    members, levels, rows, columns = control_fields.shape
    parts, peers = (lax.axis_size("mem"), lax.axis_size("row"))
    tall = column_taper.shape[0]
    at = lax.axis_index("mem").astype(jnp.int32).reshape(1)
    flip = lax.axis_index("lev").astype(jnp.int32).reshape(1)

    every = lax.all_gather(
        control_fields.reshape(members * levels * rows, columns), "mem", axis=0, tiled=True
    )
    slices = lax.all_to_all(
        taper_slices(jnp.concatenate([at, flip]), column_taper, row_taper, peers, parts), "row", 0, 0, tiled=True
    )
    sides, around, taller = background(courant_numbers, tracer_slope)
    pieces = split_columns(at, perturbations, parts)
    weights = dict(enumerate(pieces))

    def exchange(steps):
        for step in steps:
            pairs = [(i, i ^ step) for i in range(parts)]
            weights[step] = lax.ppermute(weights[step], "mem", pairs)
        return [weights[step] for step in steps]

    def hold(steps, settled):
        for step, piece in zip(steps, after([weights[step] for step in steps], settled)):
            weights[step] = piece

    settled = [*exchange((1,)), taller]
    (taller,) = after([taller], [slices])
    opposite = lax.ppermute(taller, "lev", swap("lev"))
    first_pass = columns_pass(every, slices, tall, levels, rows, 2, 1)
    half = row_part(slices, tall, settled)
    both = paired(half, lax.ppermute(half, "lev", swap("lev")), first_pass)
    (first_pass,) = after([first_pass], [both])
    row_whole = lax.all_gather(both, "mem", axis=0, tiled=False)
    hold((2, 3, 6), [first_pass])
    arrived = lax.all_to_all(first_pass, "row", 0, 0, tiled=True)
    tapered = rows_pass(joined(flip, row_whole, row_taper.shape[0], 4), arrived, [*exchange((2, 3, 6)), opposite])
    hold((4, 5, 7), [tapered])
    localized = lax.all_to_all(tapered, "row", 0, 0, tiled=True)
    exchange((4, 5, 7))
    weights = [weights[step] for step in range(parts)]
    own, rounded, first, last = weighted_sum(at, localized, weights)

    other = lax.ppermute(rounded, "lev", swap("lev"))
    outside, top, bottom = edges(rounded, *neighbours(first, last, "mem"))
    from_previous, from_next = neighbours(top, bottom, "row")
    framed = frame(outside, from_next, from_previous)
    return advect(
        flip,
        own,
        other,
        framed,
        lax.ppermute(framed, "lev", swap("lev")),
        courant_numbers,
        tracer_slope,
        sides,
        around,
        opposite,
    )


def solution(mesh):
    grid = P(None, "lev", "row", "mem")
    placed = (
        P("mem", "lev", "row", None),
        P(None, "mem", "lev", "row", None),
        P("row", None),
        P("row", None),
        grid,
        grid,
    )
    return jax.shard_map(
        on_device, mesh=mesh, in_specs=placed, out_specs=grid, check_vma=False
    )
```

```python
import jax
import jax.numpy as jnp
from jax import lax
from jax.experimental import pallas as pl
from jax.experimental.pallas import tpu as pltpu
from jax.sharding import PartitionSpec as P

STEPS = 4
BF = jnp.bfloat16
F32 = jnp.float32


def room(mebibytes):
    return pltpu.CompilerParams(vmem_limit_bytes=mebibytes * 1024 * 1024)


def in_hbm(x):
    return pltpu.with_memory_space_constraint(x, pltpu.HBM)


def shaped(shape, dtype):
    return jax.ShapeDtypeStruct(shape, dtype)


def after(arrays, settled):
    count = len(arrays)
    anywhere = pl.BlockSpec(memory_space=pl.ANY)
    return pl.pallas_call(
        lambda *refs: None,
        out_shape=[shaped(x.shape, x.dtype) for x in arrays],
        in_specs=[anywhere] * (count + len(settled)),
        out_specs=[anywhere] * count,
        input_output_aliases={i: i for i in range(count)},
        name="after",
    )(*arrays, *settled)


def slices_kernel(which_ref, column_ref, row_ref, out_ref):
    peers, height, wide = out_ref.shape
    tall = column_ref.shape[0]
    narrow = row_ref.shape[1]
    out_ref[:, :tall, :] = jnp.broadcast_to(column_ref[...][None], (peers, *column_ref.shape))
    for i in range(wide // narrow):
        piece = row_ref[(height - tall) * i : (height - tall) * (i + 1)]
        out_ref[:, tall:, i * narrow : (i + 1) * narrow] = jnp.broadcast_to(
            piece[None], (peers, *piece.shape)
        )


def taper_slices(which, column_taper, row_taper, peers, parts):
    tall, wide = (column_taper.shape[0], column_taper.shape[1] // parts)
    rows, narrow = (row_taper.shape[0], row_taper.shape[1] // parts)
    shape = (peers, tall + rows * narrow // 2 // wide, wide)
    return pl.pallas_call(
        slices_kernel,
        out_shape=shaped(shape, BF),
        grid_spec=pltpu.PrefetchScalarGridSpec(
            num_scalar_prefetch=1,
            grid=(1,),
            in_specs=[
                pl.BlockSpec((tall, wide), lambda i, which: (0, which[0])),
                pl.BlockSpec((rows // 2, narrow), lambda i, which: (which[1], which[0])),
            ],
            out_specs=pl.BlockSpec(shape, lambda i, which: (0, 0, 0)),
        ),
        compiler_params=room(6),
        name="taper_slices",
    )(which, in_hbm(column_taper), in_hbm(row_taper))


def row_part(slices, tall, settled):
    peers, height, wide = slices.shape

    def kernel(slices_ref, *refs):
        refs[-1][...] = slices_ref[:, tall:, :]

    return pl.pallas_call(
        kernel,
        out_shape=shaped((peers, height - tall, wide), BF),
        in_specs=[pl.BlockSpec(memory_space=pltpu.VMEM)]
        + [pl.BlockSpec(memory_space=pl.ANY)] * len(settled),
        compiler_params=room(4),
        name="row_part",
    )(slices, *settled)


def columns_kernel(tall, *refs):
    slices_ref, out_ref = refs[-2:]
    units, levels, rows, wide = out_ref.shape
    product = None
    for i, fields_ref in enumerate(refs[:-2]):
        depth = fields_ref.shape[1]
        count = depth // tall
        taper = slices_ref[i * count : (i + 1) * count, :tall, :].reshape(depth, 2 * wide)
        part = jnp.dot(fields_ref[...], taper, preferred_element_type=F32)
        product = part if product is None else product + part
    product = product.astype(BF)
    for member in range(units // 2):
        for side in range(2):
            part = product[
                member * levels * rows : (member + 1) * levels * rows,
                side * wide : (side + 1) * wide,
            ]
            out_ref[member * 2 + side] = part.reshape(levels, rows, wide)


def columns_pass(fields, slices, tall, levels, rows, blocks, streams):
    count, depth = fields.shape
    peers, height, wide = slices.shape
    units = 2 * count // (levels * rows)
    fields = in_hbm(fields)

    def stream(j):
        return pl.BlockSpec((count // blocks, depth // streams), lambda i: (i, j))

    return pl.pallas_call(
        lambda *refs: columns_kernel(tall, *refs),
        out_shape=shaped((units, levels, rows, wide // 2), BF),
        grid=(blocks,),
        in_specs=[stream(j) for j in range(streams)]
        + [pl.BlockSpec((peers, height, wide), lambda i: (0, 0, 0))],
        out_specs=pl.BlockSpec((units // blocks, levels, rows, wide // 2), lambda i: (i, 0, 0, 0)),
        compiler_params=room(14),
        name="columns_pass",
    )(*[fields] * streams, slices)


def pair_kernel(own_ref, other_ref, _, out_ref):
    out_ref[0] = own_ref[...]
    out_ref[1] = other_ref[...]


def paired(own, other, settled):
    whole = pl.BlockSpec(own.shape, lambda i: (0, 0, 0))
    return pl.pallas_call(
        pair_kernel,
        out_shape=shaped((2, *own.shape), own.dtype),
        grid=(1,),
        in_specs=[whole, whole, pl.BlockSpec(memory_space=pl.ANY)],
        out_specs=pl.BlockSpec((2, *own.shape), lambda i: (0, 0, 0, 0)),
        compiler_params=room(4),
        name="paired",
    )(own, other, settled)


def join_kernel(flip_ref, parts_ref, out_ref):
    parts, _, count, tall, wide = parts_ref.shape
    narrow = out_ref.shape[3] // parts
    for part in range(parts):
        at = slice(part * narrow, (part + 1) * narrow)
        for k in range(2):
            for j in range(count):
                for i in range(wide // narrow):
                    out_ref[j, k ^ flip_ref[0], i * tall : (i + 1) * tall, at] = parts_ref[
                        part, k, j, :, i * narrow : (i + 1) * narrow
                    ]


def joined(flip, taper, rows, blocks):
    parts, _, peers, tall, wide = taper.shape
    across = 2 * parts * tall * wide // rows
    count = peers // blocks
    whole = pl.pallas_call(
        join_kernel,
        out_shape=shaped((peers, 2, rows // 2, across), BF),
        grid_spec=pltpu.PrefetchScalarGridSpec(
            num_scalar_prefetch=1,
            grid=(blocks,),
            in_specs=[
                pl.BlockSpec((parts, 2, count, tall, wide), lambda i, flip: (0, 0, i, 0, 0))
            ],
            out_specs=pl.BlockSpec((count, 2, rows // 2, across), lambda i, flip: (i, 0, 0, 0)),
        ),
        compiler_params=room(6),
        name="joined",
    )(flip, in_hbm(taper))
    return whole.reshape(peers * rows, across)


def rows_kernel(taper_ref, fields_ref, *refs):
    out_ref, whole_ref = refs[-2:]
    peers, levels, rows, wide = fields_ref.shape
    for level in range(levels):
        whole_ref[:, level * wide : (level + 1) * wide] = fields_ref[:, level].reshape(
            peers * rows, wide
        )
    product = jnp.dot(taper_ref[...], whole_ref[...], preferred_element_type=F32).astype(BF)
    for level in range(levels):
        out_ref[:, level] = product[:, level * wide : (level + 1) * wide].reshape(-1, rows, wide)


def rows_pass(taper, fields, settled):
    peers, levels, rows, wide = fields.shape
    vmem = pl.BlockSpec(memory_space=pltpu.VMEM)
    return pl.pallas_call(
        rows_kernel,
        out_shape=shaped((peers, levels, rows, wide), BF),
        in_specs=[vmem, vmem] + [pl.BlockSpec(memory_space=pl.ANY)] * len(settled),
        out_specs=vmem,
        scratch_shapes=[pltpu.VMEM((peers * rows, levels * wide), BF)],
        compiler_params=room(12),
        name="rows_pass",
    )(taper, fields, *settled)


def split_kernel(at_ref, fields_ref, *out_refs):
    wide = out_refs[0].shape[-1]
    for step, out_ref in enumerate(out_refs):
        start = pl.multiple_of((at_ref[0] ^ step) * wide, wide)
        out_ref[...] = fields_ref[:, :, :, :, pl.ds(start, wide)]


def split_columns(at, fields, parts):
    shape = (*fields.shape[:-1], fields.shape[-1] // parts)
    return pl.pallas_call(
        split_kernel,
        out_shape=[shaped(shape, BF)] * parts,
        in_specs=[
            pl.BlockSpec(memory_space=pltpu.SMEM),
            pl.BlockSpec(memory_space=pltpu.VMEM),
        ],
        out_specs=[pl.BlockSpec(memory_space=pltpu.VMEM)] * parts,
        compiler_params=room(8),
        name="split_columns",
    )(at, fields)


def weight_kernel(parts, at_ref, localized_ref, *refs):
    weights = refs[:parts]
    out_ref, whole_ref, first_ref, last_ref = refs[parts:]
    variables, members, levels = weights[0].shape[:3]
    wide = localized_ref.shape[-1]
    for level in range(levels):
        for side in range(2):
            lanes = slice(side * wide, (side + 1) * wide)
            sums = [None] * variables
            for step in range(parts):
                base = (at_ref[0] ^ step) * (2 * members)
                for member in range(members):
                    field = localized_ref[base + 2 * member + side, level].astype(F32)
                    for k in range(variables):
                        term = weights[step][k, member, level, :, lanes].astype(F32) * field
                        sums[k] = term if sums[k] is None else sums[k] + term
            for k in range(variables):
                out_ref[k, level, :, lanes] = sums[k]
                rounded = sums[k].astype(BF)
                whole_ref[k, level, :, lanes] = rounded
                (first_ref, last_ref)[side][k, level] = rounded


def weighted_sum(at, localized, weights):
    variables, _, levels, rows, wide = weights[0].shape
    shape = (variables, levels, rows, wide)
    edge = (variables, levels, rows, wide // 2)
    vmem = pl.BlockSpec(memory_space=pltpu.VMEM)
    return pl.pallas_call(
        lambda *refs: weight_kernel(len(weights), *refs),
        out_shape=[shaped(shape, F32), shaped(shape, BF), shaped(edge, BF), shaped(edge, BF)],
        in_specs=[pl.BlockSpec(memory_space=pltpu.SMEM)] + [vmem] * (1 + len(weights)),
        out_specs=[vmem] * 4,
        compiler_params=room(8),
        name="weighted_sum",
    )(at, localized, *weights)


def beside(from_left, from_right):
    lane = lax.broadcasted_iota(jnp.int32, from_left.shape, from_left.ndim - 1)
    wide = from_left.shape[-1]
    none = jnp.zeros_like(from_left)
    kept = jnp.where(lane >= wide - STEPS, from_left, none)
    return jnp.where(lane < STEPS, from_right, kept)


def above_below(from_next, from_previous):
    row = lax.broadcasted_iota(jnp.int32, from_next.shape, from_next.ndim - 2)
    return jnp.where(row < STEPS, from_next, from_previous)


def edges_kernel(body_ref, left_ref, right_ref, sides_ref, top_ref, bottom_ref):
    variables, levels, rows, wide = body_ref.shape
    for k in range(variables):
        for level in range(levels):
            sides = beside(left_ref[k, level].astype(F32), right_ref[k, level].astype(F32))
            sides_ref[k, level] = sides.astype(BF)
            for at, out_ref in ((slice(0, 8), top_ref), (slice(rows - 8, rows), bottom_ref)):
                out_ref[k, level, :, :wide] = body_ref[k, level, at]
                out_ref[k, level, :, wide:] = sides_ref[k, level, at]


def edges(body, left, right):
    variables, levels, rows, wide = body.shape
    strip = shaped((variables, levels, 8, wide + left.shape[-1]), BF)
    return pl.pallas_call(
        edges_kernel,
        out_shape=[shaped(left.shape, BF), strip, strip],
        compiler_params=room(4),
        name="edges",
    )(body, left, right)


def frame_kernel(sides_ref, next_ref, previous_ref, out_ref):
    variables, levels, rows, wide = sides_ref.shape
    for k in range(variables):
        for level in range(levels):
            out_ref[k, level, :rows] = sides_ref[k, level]
            around = above_below(
                next_ref[k, level].astype(F32), previous_ref[k, level].astype(F32)
            ).astype(BF)
            for i in range(around.shape[1] // wide):
                at = rows + 8 * i
                out_ref[k, level, at : at + 8] = around[:, i * wide : (i + 1) * wide]


def frame(sides, from_next, from_previous):
    variables, levels, rows, wide = sides.shape
    tall = rows + 8 * (from_next.shape[-1] // wide)
    return pl.pallas_call(
        frame_kernel,
        out_shape=shaped((variables, levels, tall, wide), BF),
        compiler_params=room(4),
        name="frame",
    )(sides, from_next, from_previous)


def advect_kernel(*refs):
    (
        flip_ref,
        own_ref,
        other_ref,
        frame_ref,
        other_frame_ref,
        courant_ref,
        slope_ref,
        beside_ref,
        around_ref,
        opposite_ref,
        out_ref,
        first_ref,
        second_ref,
        terms_ref,
        held_ref,
        arrival,
    ) = refs
    fetch = pltpu.make_async_copy(own_ref, held_ref, arrival)
    fetch.start()
    variables, levels, rows, wide = own_ref.shape
    deep, tall, full = first_ref.shape[1:]
    flip = flip_ref[0]
    sign = (1 - 2 * flip).astype(F32)
    directions = courant_ref.shape[0]

    def local(level):
        return jnp.where(flip == 1, levels - 1 - level, level)

    for level in range(deep):
        at = local(level % levels)
        mine = level < levels
        for k in range(variables):
            around_of = frame_ref if mine else other_frame_ref
            if not mine:
                first_ref[k, level, :rows, :wide] = other_ref[k, at].astype(F32)
            first_ref[k, level, :rows, wide:] = around_of[k, at, :rows].astype(F32)
            for i in range(full // (full - wide)):
                lanes = slice(i * (full - wide), (i + 1) * (full - wide))
                strip = around_of[k, at, rows + 8 * i : rows + 8 * (i + 1)]
                first_ref[k, level, rows:, lanes] = strip.astype(F32)
        planes = []
        for a in range(directions + slope_ref.shape[0]):
            if mine:
                body = courant_ref[a, at] if a < directions else slope_ref[a - directions, at]
                upper = jnp.concatenate([body, beside_ref[a, at].astype(F32)], axis=1)
                plane = jnp.concatenate([upper, around_ref[a, at].astype(F32)], axis=0)
            else:
                plane = opposite_ref[a, at].astype(F32)
            planes.append(plane)
        planes[0] = planes[0] * sign
        kept = 1.0 - sum(jnp.abs(c) for c in planes[:directions])
        terms_ref[0, level] = kept
        for a in range(directions):
            terms_ref[1 + 2 * a, level] = jnp.maximum(planes[a], 0.0)
            terms_ref[2 + 2 * a, level] = -jnp.minimum(planes[a], 0.0)
        for a in range(directions, len(planes)):
            terms_ref[1 + directions + a, level] = planes[a]

    fetch.wait()
    for level in range(levels):
        for k in range(variables):
            first_ref[k, level, :rows, :wide] = held_ref[k, local(level)]

    old_ref, new_ref = (first_ref, second_ref)
    for step in range(STEPS):
        reached = min(deep, levels + STEPS - 1 - step)
        last = step == STEPS - 1
        for level in range(reached):
            states = [old_ref[k, level] for k in range(variables)]
            for k in range(variables):
                state = states[k]
                total = terms_ref[0, level] * state
                if level > 0:
                    total = total + terms_ref[1, level] * old_ref[k, level - 1]
                if level + 1 < deep:
                    total = total + terms_ref[2, level] * old_ref[k, level + 1]
                total = total + terms_ref[3, level] * pltpu.roll(state, 1, 0)
                total = total + terms_ref[4, level] * pltpu.roll(state, tall - 1, 0)
                total = total + terms_ref[5, level] * pltpu.roll(state, 1, 1)
                total = total + terms_ref[6, level] * pltpu.roll(state, full - 1, 1)
                if k == 2:
                    total = total - (states[0] * terms_ref[7, level] + states[1] * terms_ref[8, level])
                if last:
                    out_ref[k, local(level)] = total[:rows, :wide]
                else:
                    new_ref[k, level] = total
        old_ref, new_ref = (new_ref, old_ref)


def advect(flip, *arrays):
    variables, levels, rows, wide = arrays[0].shape
    tall, full = (rows + 8, wide + arrays[2].shape[-1])
    vmem = pl.BlockSpec(memory_space=pltpu.VMEM)
    state = pltpu.VMEM((variables, 2 * levels, tall, full), F32)
    return pl.pallas_call(
        advect_kernel,
        out_shape=shaped((variables, levels, rows, wide), F32),
        in_specs=[pl.BlockSpec(memory_space=pltpu.SMEM), pl.BlockSpec(memory_space=pl.ANY)]
        + [vmem] * (len(arrays) - 1),
        out_specs=vmem,
        scratch_shapes=[
            state,
            state,
            pltpu.VMEM((9, 2 * levels, tall, full), F32),
            pltpu.VMEM((variables, levels, rows, wide), F32),
            pltpu.SemaphoreType.DMA(()),
        ],
        compiler_params=room(14),
        name="advect",
    )(flip, *arrays)


def chain(axis, step):
    size = lax.axis_size(axis)
    return [(i, i + step) for i in range(size) if 0 <= i + step < size]


def swap(axis):
    return [(0, 1), (1, 0)]


def neighbours(first, last, axis):
    from_left = lax.ppermute(last, axis, chain(axis, 1))
    from_right = lax.ppermute(first, axis, chain(axis, -1))
    return from_left, from_right


def background(courant_numbers, tracer_slope):
    whole = jnp.concatenate([courant_numbers, tracer_slope], axis=0).astype(BF)
    half = whole.shape[-1] // 2
    sides = beside(*neighbours(whole[..., :half], whole[..., half:], "mem"))
    wider = jnp.concatenate([whole, sides], axis=-1)
    from_previous, from_next = neighbours(wider[:, :, :8], wider[:, :, -8:], "row")
    around = above_below(from_next, from_previous)
    return sides, around, jnp.concatenate([wider, around], axis=2)


def on_device(
    control_fields, perturbations, column_taper, row_taper, courant_numbers, tracer_slope
):
    members, levels, rows, columns = control_fields.shape
    parts, peers = (lax.axis_size("mem"), lax.axis_size("row"))
    tall = column_taper.shape[0]
    at = lax.axis_index("mem").astype(jnp.int32).reshape(1)
    flip = lax.axis_index("lev").astype(jnp.int32).reshape(1)

    every = lax.all_gather(
        control_fields.reshape(members * levels * rows, columns), "mem", axis=0, tiled=True
    )
    slices = lax.all_to_all(
        taper_slices(jnp.concatenate([at, flip]), column_taper, row_taper, peers, parts), "row", 0, 0, tiled=True
    )
    sides, around, taller = background(courant_numbers, tracer_slope)
    pieces = split_columns(at, perturbations, parts)
    weights = dict(enumerate(pieces))

    def exchange(steps):
        for step in steps:
            pairs = [(i, i ^ step) for i in range(parts)]
            weights[step] = lax.ppermute(weights[step], "mem", pairs)
        return [weights[step] for step in steps]

    def hold(steps, settled):
        for step, piece in zip(steps, after([weights[step] for step in steps], settled)):
            weights[step] = piece

    settled = [*exchange((1,)), taller]
    (taller,) = after([taller], [slices])
    opposite = lax.ppermute(taller, "lev", swap("lev"))
    first_pass = columns_pass(every, slices, tall, levels, rows, 2, 1)
    half = row_part(slices, tall, settled)
    both = paired(half, lax.ppermute(half, "lev", swap("lev")), first_pass)
    (first_pass,) = after([first_pass], [both])
    row_whole = lax.all_gather(both, "mem", axis=0, tiled=False)
    hold((2, 3, 6), [first_pass])
    arrived = lax.all_to_all(first_pass, "row", 0, 0, tiled=True)
    tapered = rows_pass(joined(flip, row_whole, row_taper.shape[0], 4), arrived, [*exchange((2, 3, 6)), opposite])
    hold((4, 5, 7), [tapered])
    localized = lax.all_to_all(tapered, "row", 0, 0, tiled=True)
    exchange((4, 5, 7))
    weights = [weights[step] for step in range(parts)]
    own, rounded, first, last = weighted_sum(at, localized, weights)

    other = lax.ppermute(rounded, "lev", swap("lev"))
    outside, top, bottom = edges(rounded, *neighbours(first, last, "mem"))
    from_previous, from_next = neighbours(top, bottom, "row")
    framed = frame(outside, from_next, from_previous)
    return advect(
        flip,
        own,
        other,
        framed,
        lax.ppermute(framed, "lev", swap("lev")),
        courant_numbers,
        tracer_slope,
        sides,
        around,
        opposite,
    )


def solution(mesh):
    grid = P(None, "lev", "row", "mem")
    placed = (
        P("mem", "lev", "row", None),
        P(None, "mem", "lev", "row", None),
        P("row", None),
        P("row", None),
        grid,
        grid,
    )
    return jax.shard_map(
        on_device, mesh=mesh, in_specs=placed, out_specs=grid, check_vma=False
    )
```

```python
import jax
import jax.numpy as jnp
from jax import lax
from jax.experimental import pallas as pl
from jax.experimental.pallas import tpu as pltpu
from jax.sharding import PartitionSpec as P

STEPS = 4
BF = jnp.bfloat16
F32 = jnp.float32


def room(mebibytes):
    return pltpu.CompilerParams(vmem_limit_bytes=mebibytes * 1024 * 1024)


def in_hbm(x):
    return pltpu.with_memory_space_constraint(x, pltpu.HBM)


def shaped(shape, dtype):
    return jax.ShapeDtypeStruct(shape, dtype)


def after(arrays, settled):
    count = len(arrays)
    anywhere = pl.BlockSpec(memory_space=pl.ANY)
    return pl.pallas_call(
        lambda *refs: None,
        out_shape=[shaped(x.shape, x.dtype) for x in arrays],
        in_specs=[anywhere] * (count + len(settled)),
        out_specs=[anywhere] * count,
        input_output_aliases={i: i for i in range(count)},
        name="after",
    )(*arrays, *settled)


def slices_kernel(which_ref, column_ref, row_ref, out_ref):
    peers, height, wide = out_ref.shape
    tall = column_ref.shape[0]
    narrow = row_ref.shape[1]
    out_ref[:, :tall, :] = jnp.broadcast_to(column_ref[...][None], (peers, *column_ref.shape))
    for i in range(wide // narrow):
        piece = row_ref[(height - tall) * i : (height - tall) * (i + 1)]
        out_ref[:, tall:, i * narrow : (i + 1) * narrow] = jnp.broadcast_to(
            piece[None], (peers, *piece.shape)
        )


def taper_slices(which, column_taper, row_taper, peers, parts):
    tall, wide = (column_taper.shape[0], column_taper.shape[1] // parts)
    rows, narrow = (row_taper.shape[0], row_taper.shape[1] // parts)
    shape = (peers, tall + rows * narrow // 2 // wide, wide)
    return pl.pallas_call(
        slices_kernel,
        out_shape=shaped(shape, BF),
        grid_spec=pltpu.PrefetchScalarGridSpec(
            num_scalar_prefetch=1,
            grid=(1,),
            in_specs=[
                pl.BlockSpec((tall, wide), lambda i, which: (0, which[0])),
                pl.BlockSpec((rows // 2, narrow), lambda i, which: (which[1], which[0])),
            ],
            out_specs=pl.BlockSpec(shape, lambda i, which: (0, 0, 0)),
        ),
        compiler_params=room(6),
        name="taper_slices",
    )(which, in_hbm(column_taper), in_hbm(row_taper))


def row_part(slices, tall, settled):
    peers, height, wide = slices.shape

    def kernel(slices_ref, *refs):
        refs[-1][...] = slices_ref[:, tall:, :]

    return pl.pallas_call(
        kernel,
        out_shape=shaped((peers, height - tall, wide), BF),
        in_specs=[pl.BlockSpec(memory_space=pltpu.VMEM)]
        + [pl.BlockSpec(memory_space=pl.ANY)] * len(settled),
        compiler_params=room(4),
        name="row_part",
    )(slices, *settled)


def columns_kernel(tall, *refs):
    slices_ref, out_ref = refs[-2:]
    units, levels, rows, wide = out_ref.shape
    product = None
    for i, fields_ref in enumerate(refs[:-2]):
        depth = fields_ref.shape[1]
        count = depth // tall
        taper = slices_ref[i * count : (i + 1) * count, :tall, :].reshape(depth, 2 * wide)
        part = jnp.dot(fields_ref[...], taper, preferred_element_type=F32)
        product = part if product is None else product + part
    product = product.astype(BF)
    for member in range(units // 2):
        for side in range(2):
            part = product[
                member * levels * rows : (member + 1) * levels * rows,
                side * wide : (side + 1) * wide,
            ]
            out_ref[member * 2 + side] = part.reshape(levels, rows, wide)


def columns_pass(fields, slices, tall, levels, rows, blocks, streams):
    count, depth = fields.shape
    peers, height, wide = slices.shape
    units = 2 * count // (levels * rows)
    fields = in_hbm(fields)

    def stream(j):
        return pl.BlockSpec((count // blocks, depth // streams), lambda i: (i, j))

    return pl.pallas_call(
        lambda *refs: columns_kernel(tall, *refs),
        out_shape=shaped((units, levels, rows, wide // 2), BF),
        grid=(blocks,),
        in_specs=[stream(j) for j in range(streams)]
        + [pl.BlockSpec((peers, height, wide), lambda i: (0, 0, 0))],
        out_specs=pl.BlockSpec((units // blocks, levels, rows, wide // 2), lambda i: (i, 0, 0, 0)),
        compiler_params=room(14),
        name="columns_pass",
    )(*[fields] * streams, slices)


def pair_kernel(own_ref, other_ref, _, out_ref):
    out_ref[0] = own_ref[...]
    out_ref[1] = other_ref[...]


def paired(own, other, settled):
    whole = pl.BlockSpec(own.shape, lambda i: (0, 0, 0))
    return pl.pallas_call(
        pair_kernel,
        out_shape=shaped((2, *own.shape), own.dtype),
        grid=(1,),
        in_specs=[whole, whole, pl.BlockSpec(memory_space=pl.ANY)],
        out_specs=pl.BlockSpec((2, *own.shape), lambda i: (0, 0, 0, 0)),
        compiler_params=room(4),
        name="paired",
    )(own, other, settled)


def join_kernel(flip_ref, parts_ref, out_ref):
    parts, _, count, tall, wide = parts_ref.shape
    narrow = out_ref.shape[3] // parts
    for part in range(parts):
        at = slice(part * narrow, (part + 1) * narrow)
        for k in range(2):
            for j in range(count):
                for i in range(wide // narrow):
                    out_ref[j, k ^ flip_ref[0], i * tall : (i + 1) * tall, at] = parts_ref[
                        part, k, j, :, i * narrow : (i + 1) * narrow
                    ]


def joined(flip, taper, rows, blocks):
    parts, _, peers, tall, wide = taper.shape
    across = 2 * parts * tall * wide // rows
    count = peers // blocks
    whole = pl.pallas_call(
        join_kernel,
        out_shape=shaped((peers, 2, rows // 2, across), BF),
        grid_spec=pltpu.PrefetchScalarGridSpec(
            num_scalar_prefetch=1,
            grid=(blocks,),
            in_specs=[
                pl.BlockSpec((parts, 2, count, tall, wide), lambda i, flip: (0, 0, i, 0, 0))
            ],
            out_specs=pl.BlockSpec((count, 2, rows // 2, across), lambda i, flip: (i, 0, 0, 0)),
        ),
        compiler_params=room(6),
        name="joined",
    )(flip, in_hbm(taper))
    return whole.reshape(peers * rows, across)


def rows_kernel(taper_ref, fields_ref, *refs):
    out_ref, whole_ref = refs[-2:]
    peers, levels, rows, wide = fields_ref.shape
    for level in range(levels):
        whole_ref[:, level * wide : (level + 1) * wide] = fields_ref[:, level].reshape(
            peers * rows, wide
        )
    product = jnp.dot(taper_ref[...], whole_ref[...], preferred_element_type=F32).astype(BF)
    for level in range(levels):
        out_ref[:, level] = product[:, level * wide : (level + 1) * wide].reshape(-1, rows, wide)


def rows_pass(taper, fields, settled):
    peers, levels, rows, wide = fields.shape
    vmem = pl.BlockSpec(memory_space=pltpu.VMEM)
    return pl.pallas_call(
        rows_kernel,
        out_shape=shaped((peers, levels, rows, wide), BF),
        in_specs=[vmem, vmem] + [pl.BlockSpec(memory_space=pl.ANY)] * len(settled),
        out_specs=vmem,
        scratch_shapes=[pltpu.VMEM((peers * rows, levels * wide), BF)],
        compiler_params=room(12),
        name="rows_pass",
    )(taper, fields, *settled)


def split_kernel(at_ref, fields_ref, *out_refs):
    wide = out_refs[0].shape[-1]
    for step, out_ref in enumerate(out_refs):
        start = pl.multiple_of((at_ref[0] ^ step) * wide, wide)
        out_ref[...] = fields_ref[:, :, :, :, pl.ds(start, wide)]


def split_columns(at, fields, parts):
    shape = (*fields.shape[:-1], fields.shape[-1] // parts)
    return pl.pallas_call(
        split_kernel,
        out_shape=[shaped(shape, BF)] * parts,
        in_specs=[
            pl.BlockSpec(memory_space=pltpu.SMEM),
            pl.BlockSpec(memory_space=pltpu.VMEM),
        ],
        out_specs=[pl.BlockSpec(memory_space=pltpu.VMEM)] * parts,
        compiler_params=room(8),
        name="split_columns",
    )(at, fields)


def weight_kernel(parts, at_ref, localized_ref, *refs):
    weights = refs[:parts]
    out_ref, whole_ref, first_ref, last_ref = refs[parts:]
    variables, members, levels = weights[0].shape[:3]
    wide = localized_ref.shape[-1]
    for level in range(levels):
        for side in range(2):
            lanes = slice(side * wide, (side + 1) * wide)
            sums = [None] * variables
            for step in range(parts):
                base = (at_ref[0] ^ step) * (2 * members)
                for member in range(members):
                    field = localized_ref[base + 2 * member + side, level].astype(F32)
                    for k in range(variables):
                        term = weights[step][k, member, level, :, lanes].astype(F32) * field
                        sums[k] = term if sums[k] is None else sums[k] + term
            for k in range(variables):
                out_ref[k, level, :, lanes] = sums[k]
                rounded = sums[k].astype(BF)
                whole_ref[k, level, :, lanes] = rounded
                (first_ref, last_ref)[side][k, level] = rounded


def weighted_sum(at, localized, weights):
    variables, _, levels, rows, wide = weights[0].shape
    shape = (variables, levels, rows, wide)
    edge = (variables, levels, rows, wide // 2)
    vmem = pl.BlockSpec(memory_space=pltpu.VMEM)
    return pl.pallas_call(
        lambda *refs: weight_kernel(len(weights), *refs),
        out_shape=[shaped(shape, F32), shaped(shape, BF), shaped(edge, BF), shaped(edge, BF)],
        in_specs=[pl.BlockSpec(memory_space=pltpu.SMEM)] + [vmem] * (1 + len(weights)),
        out_specs=[vmem] * 4,
        compiler_params=room(8),
        name="weighted_sum",
    )(at, localized, *weights)


def beside(from_left, from_right):
    lane = lax.broadcasted_iota(jnp.int32, from_left.shape, from_left.ndim - 1)
    wide = from_left.shape[-1]
    none = jnp.zeros_like(from_left)
    kept = jnp.where(lane >= wide - STEPS, from_left, none)
    return jnp.where(lane < STEPS, from_right, kept)


def above_below(from_next, from_previous):
    row = lax.broadcasted_iota(jnp.int32, from_next.shape, from_next.ndim - 2)
    return jnp.where(row < STEPS, from_next, from_previous)


def edges_kernel(body_ref, left_ref, right_ref, sides_ref, top_ref, bottom_ref):
    variables, levels, rows, wide = body_ref.shape
    for k in range(variables):
        for level in range(levels):
            sides = beside(left_ref[k, level].astype(F32), right_ref[k, level].astype(F32))
            sides_ref[k, level] = sides.astype(BF)
            for at, out_ref in ((slice(0, 8), top_ref), (slice(rows - 8, rows), bottom_ref)):
                out_ref[k, level, :, :wide] = body_ref[k, level, at]
                out_ref[k, level, :, wide:] = sides_ref[k, level, at]


def edges(body, left, right):
    variables, levels, rows, wide = body.shape
    strip = shaped((variables, levels, 8, wide + left.shape[-1]), BF)
    return pl.pallas_call(
        edges_kernel,
        out_shape=[shaped(left.shape, BF), strip, strip],
        compiler_params=room(4),
        name="edges",
    )(body, left, right)


def frame_kernel(sides_ref, next_ref, previous_ref, out_ref):
    variables, levels, rows, wide = sides_ref.shape
    for k in range(variables):
        for level in range(levels):
            out_ref[k, level, :rows] = sides_ref[k, level]
            around = above_below(
                next_ref[k, level].astype(F32), previous_ref[k, level].astype(F32)
            ).astype(BF)
            for i in range(around.shape[1] // wide):
                at = rows + 8 * i
                out_ref[k, level, at : at + 8] = around[:, i * wide : (i + 1) * wide]


def frame(sides, from_next, from_previous):
    variables, levels, rows, wide = sides.shape
    tall = rows + 8 * (from_next.shape[-1] // wide)
    return pl.pallas_call(
        frame_kernel,
        out_shape=shaped((variables, levels, tall, wide), BF),
        compiler_params=room(4),
        name="frame",
    )(sides, from_next, from_previous)


def advect_kernel(*refs):
    (
        flip_ref,
        own_ref,
        other_ref,
        frame_ref,
        other_frame_ref,
        courant_ref,
        slope_ref,
        beside_ref,
        around_ref,
        opposite_ref,
        out_ref,
        first_ref,
        second_ref,
        terms_ref,
        held_ref,
        arrival,
    ) = refs
    fetch = pltpu.make_async_copy(own_ref, held_ref, arrival)
    fetch.start()
    variables, levels, rows, wide = own_ref.shape
    deep, tall, full = first_ref.shape[1:]
    flip = flip_ref[0]
    sign = (1 - 2 * flip).astype(F32)
    directions = courant_ref.shape[0]

    def local(level):
        return jnp.where(flip == 1, levels - 1 - level, level)

    for level in range(deep):
        at = local(level % levels)
        mine = level < levels
        for k in range(variables):
            around_of = frame_ref if mine else other_frame_ref
            if not mine:
                first_ref[k, level, :rows, :wide] = other_ref[k, at].astype(F32)
            first_ref[k, level, :rows, wide:] = around_of[k, at, :rows].astype(F32)
            for i in range(full // (full - wide)):
                lanes = slice(i * (full - wide), (i + 1) * (full - wide))
                strip = around_of[k, at, rows + 8 * i : rows + 8 * (i + 1)]
                first_ref[k, level, rows:, lanes] = strip.astype(F32)
        planes = []
        for a in range(directions + slope_ref.shape[0]):
            if mine:
                body = courant_ref[a, at] if a < directions else slope_ref[a - directions, at]
                upper = jnp.concatenate([body, beside_ref[a, at].astype(F32)], axis=1)
                plane = jnp.concatenate([upper, around_ref[a, at].astype(F32)], axis=0)
            else:
                plane = opposite_ref[a, at].astype(F32)
            planes.append(plane)
        planes[0] = planes[0] * sign
        kept = 1.0 - sum(jnp.abs(c) for c in planes[:directions])
        terms_ref[0, level] = kept
        for a in range(directions):
            terms_ref[1 + 2 * a, level] = jnp.maximum(planes[a], 0.0)
            terms_ref[2 + 2 * a, level] = -jnp.minimum(planes[a], 0.0)
        for a in range(directions, len(planes)):
            terms_ref[1 + directions + a, level] = planes[a]

    fetch.wait()
    for level in range(levels):
        for k in range(variables):
            first_ref[k, level, :rows, :wide] = held_ref[k, local(level)]

    old_ref, new_ref = (first_ref, second_ref)
    for step in range(STEPS):
        reached = min(deep, levels + STEPS - 1 - step)
        last = step == STEPS - 1
        for level in range(reached):
            states = [old_ref[k, level] for k in range(variables)]
            for k in range(variables):
                state = states[k]
                total = terms_ref[0, level] * state
                if level > 0:
                    total = total + terms_ref[1, level] * old_ref[k, level - 1]
                if level + 1 < deep:
                    total = total + terms_ref[2, level] * old_ref[k, level + 1]
                total = total + terms_ref[3, level] * pltpu.roll(state, 1, 0)
                total = total + terms_ref[4, level] * pltpu.roll(state, tall - 1, 0)
                total = total + terms_ref[5, level] * pltpu.roll(state, 1, 1)
                total = total + terms_ref[6, level] * pltpu.roll(state, full - 1, 1)
                if k == 2:
                    total = total - (states[0] * terms_ref[7, level] + states[1] * terms_ref[8, level])
                if last:
                    out_ref[k, local(level)] = total[:rows, :wide]
                else:
                    new_ref[k, level] = total
        old_ref, new_ref = (new_ref, old_ref)


def advect(flip, *arrays):
    variables, levels, rows, wide = arrays[0].shape
    tall, full = (rows + 8, wide + arrays[2].shape[-1])
    vmem = pl.BlockSpec(memory_space=pltpu.VMEM)
    state = pltpu.VMEM((variables, 2 * levels, tall, full), F32)
    return pl.pallas_call(
        advect_kernel,
        out_shape=shaped((variables, levels, rows, wide), F32),
        in_specs=[pl.BlockSpec(memory_space=pltpu.SMEM), pl.BlockSpec(memory_space=pl.ANY)]
        + [vmem] * (len(arrays) - 1),
        out_specs=vmem,
        scratch_shapes=[
            state,
            state,
            pltpu.VMEM((9, 2 * levels, tall, full), F32),
            pltpu.VMEM((variables, levels, rows, wide), F32),
            pltpu.SemaphoreType.DMA(()),
        ],
        compiler_params=room(14),
        name="advect",
    )(flip, *arrays)


def chain(axis, step):
    size = lax.axis_size(axis)
    return [(i, i + step) for i in range(size) if 0 <= i + step < size]


def swap(axis):
    return [(0, 1), (1, 0)]


def neighbours(first, last, axis):
    from_left = lax.ppermute(last, axis, chain(axis, 1))
    from_right = lax.ppermute(first, axis, chain(axis, -1))
    return from_left, from_right


def background(courant_numbers, tracer_slope):
    whole = jnp.concatenate([courant_numbers, tracer_slope], axis=0).astype(BF)
    half = whole.shape[-1] // 2
    sides = beside(*neighbours(whole[..., :half], whole[..., half:], "mem"))
    wider = jnp.concatenate([whole, sides], axis=-1)
    from_previous, from_next = neighbours(wider[:, :, :8], wider[:, :, -8:], "row")
    around = above_below(from_next, from_previous)
    return sides, around, jnp.concatenate([wider, around], axis=2)


def on_device(
    control_fields, perturbations, column_taper, row_taper, courant_numbers, tracer_slope
):
    members, levels, rows, columns = control_fields.shape
    parts, peers = (lax.axis_size("mem"), lax.axis_size("row"))
    tall = column_taper.shape[0]
    at = lax.axis_index("mem").astype(jnp.int32).reshape(1)
    flip = lax.axis_index("lev").astype(jnp.int32).reshape(1)

    every = lax.all_gather(
        control_fields.reshape(members * levels * rows, columns), "mem", axis=0, tiled=True
    )
    slices = lax.all_to_all(
        taper_slices(jnp.concatenate([at, flip]), column_taper, row_taper, peers, parts), "row", 0, 0, tiled=True
    )
    sides, around, taller = background(courant_numbers, tracer_slope)
    pieces = split_columns(at, perturbations, parts)
    weights = dict(enumerate(pieces))

    def exchange(steps):
        for step in steps:
            pairs = [(i, i ^ step) for i in range(parts)]
            weights[step] = lax.ppermute(weights[step], "mem", pairs)
        return [weights[step] for step in steps]

    def hold(steps, settled):
        for step, piece in zip(steps, after([weights[step] for step in steps], settled)):
            weights[step] = piece

    settled = [*exchange((1,)), taller]
    (taller,) = after([taller], [slices])
    opposite = lax.ppermute(taller, "lev", swap("lev"))
    first_pass = columns_pass(every, slices, tall, levels, rows, 2, 1)
    half = row_part(slices, tall, settled)
    both = paired(half, lax.ppermute(half, "lev", swap("lev")), first_pass)
    (first_pass,) = after([first_pass], [both])
    row_whole = lax.all_gather(both, "mem", axis=0, tiled=False)
    hold((2, 3, 6), [first_pass])
    arrived = lax.all_to_all(first_pass, "row", 0, 0, tiled=True)
    tapered = rows_pass(joined(flip, row_whole, row_taper.shape[0], 2), arrived, [*exchange((2, 3, 6)), opposite])
    hold((4, 5, 7), [tapered])
    localized = lax.all_to_all(tapered, "row", 0, 0, tiled=True)
    exchange((4, 5, 7))
    weights = [weights[step] for step in range(parts)]
    own, rounded, first, last = weighted_sum(at, localized, weights)

    other = lax.ppermute(rounded, "lev", swap("lev"))
    outside, top, bottom = edges(rounded, *neighbours(first, last, "mem"))
    from_previous, from_next = neighbours(top, bottom, "row")
    framed = frame(outside, from_next, from_previous)
    return advect(
        flip,
        own,
        other,
        framed,
        lax.ppermute(framed, "lev", swap("lev")),
        courant_numbers,
        tracer_slope,
        sides,
        around,
        opposite,
    )


def solution(mesh):
    grid = P(None, "lev", "row", "mem")
    placed = (
        P("mem", "lev", "row", None),
        P(None, "mem", "lev", "row", None),
        P("row", None),
        P("row", None),
        grid,
        grid,
    )
    return jax.shard_map(
        on_device, mesh=mesh, in_specs=placed, out_specs=grid, check_vma=False
    )
```
